256 devices in a mesh: group: 8 (over y_hi, x), shard: 32 (over y_lo, z, core).
Axes of the slice: x: 4, y: 4 (y_hi: 2, y_lo: 2; y = y_hi * 2 + y_lo), z: 8, core: 2. Of those that a mesh axis runs over, the one named last changes fastest.
Arguments:
- entity_rows: float32 [262144, 200], P(('group', 'shard')), may hold values from -4 to 4
- entity_state: float32 [262144], P(('group', 'shard')), may hold values from 0.5 to 4
- relation_rows: float32 [1387, 200], replicated, may hold values from -6 to 6
- relation_state: float32 [1387], replicated, may hold values from 16 to 160
- conv_weight: bfloat16 [32, 3, 3], replicated, may hold values from -2 to 2
- conv_bias: float32 [32], replicated, may hold values from -3 to 3
- fc_weight: bfloat16 [10368, 200], replicated, may hold values from -0.0625 to 0.0625
- fc_bias: float32 [200], replicated, may hold values from -3 to 3
- head_ids: int32 [2, 32768], P(None, ('group', 'shard')), may hold values from 0 to 1023
- rel_ids: int32 [2, 32768], P(None, ('group', 'shard')), may hold values from 0 to 1386
- tail_ids: int32 [2, 32768], P(None, ('group', 'shard')), may hold values from 0 to 1023
- neg_ids: int32 [2, 8192], P(None, ('group', 'shard')), may hold values from 0 to 1023
Outputs:
- new_entity_rows: float32 [262144, 200], P(('group', 'shard'))
- new_entity_state: float32 [262144], P(('group', 'shard'))
- new_relation_rows: float32 [1387, 200], replicated
- new_relation_state: float32 [1387], replicated
The draws below stay inside these ranges and needn't reach their ends.
All inputs are finite; a program needn't handle non-finite values.
Results may differ from the reference program's by a relative error of at most 0.002.
Values may be sent and summed in bfloat16 or wider, within the bound.
A program may use at most 128 MiB of HBM per device.

```python
import math
import jax
import jax.numpy as jnp
import numpy as np
from jax import lax

EMB_H = 10
EMB_W = 20
D = 200
FILTERS = 32
FLAT = 10368
REL = 1387
ENT_DEV = 1024
TRI_DEV = 128
NEG_DEV = 32
ROUNDS = 2
NEG_SPAN = 1024
ENTITIES = 262144
TRI_ALL = 32768
NEG_ALL = 8192
N_GROUP = 8
N_SHARD = 32


def set_ends(array, rng, least, top_value):
    spot = [jax.random.randint(jax.random.fold_in(rng, axis), (), 0, length) for axis, length in enumerate(array.shape)]
    longest = array.shape.index(max(array.shape))
    next_to = spot[:longest] + [(spot[longest] + 1) % array.shape[longest]] + spot[longest + 1:]
    return array.at[tuple(spot)].set(least).at[tuple(next_to)].set(top_value)


def block_levels(stream_key, shape, cuts, least, top_value):
    gain = 1.0
    for position, parts in cuts:
        draws = jax.random.uniform(jax.random.fold_in(jax.random.fold_in(stream_key, 6), position), (parts,), jnp.float32, least / len(cuts), top_value / len(cuts))
        gain = gain * jnp.repeat(jnp.exp(draws), shape[position] // parts).reshape((-1,) + (1,) * (len(shape) - 1 - position))
    return gain


def rank_table(number_of, skew):
    weights = [(1 << 20) // math.isqrt(standing ** skew) + 1 for standing in range(1, number_of + 1)]
    scale = 1 + sum(weights) // (1 << 30)
    return np.cumsum(np.array([max(1, weight // scale) for weight in weights]))


def ranked_ids(key, extent, count, lean):
    listing = rank_table(count, lean)
    pick = jax.random.randint(jax.random.fold_in(key, 1), extent, 0, int(listing[count - 1]))
    rank = jnp.searchsorted(jnp.asarray(listing, jnp.int32), pick, side="right")
    return jax.random.permutation(jax.random.fold_in(key, 2), count)[rank].astype(jnp.int32)


def normal_values(stream_key, extent, deviation, most, cuts=(), kind=jnp.bfloat16):
    factor_of = block_levels(stream_key, extent, cuts, -0.22, 0.18) if cuts else 1.0
    drawn = jax.random.normal(stream_key, extent, jnp.float32) * deviation * factor_of
    return jnp.minimum(jnp.maximum(drawn, -most), most).astype(kind)


def setup_inputs(seed: int = 0) -> dict:
    key_list = jax.random.split(jax.random.key(seed), 13)
    return {
        "entity_rows": normal_values(key_list[0], (ENTITIES, D), 0.3, 4.0, ((0, 256),), jnp.float32),
        "entity_state": jnp.clip(jnp.exp(math.log(4.0) - 2.0794415 * jax.random.uniform(key_list[1], (ENTITIES,), jnp.float32) ** block_levels(key_list[1], (ENTITIES,), ((0, 256),), -0.2, 0.2)), 0.5, 4.0),
        "relation_rows": normal_values(key_list[2], (REL, D), 0.5, 6.0, (), jnp.float32),
        "relation_state": jnp.clip(jnp.exp(jax.random.uniform(key_list[3], (REL,), jnp.float32, math.log(16.0), math.log(160.0))), 16.0, 160.0),
        "conv_weight": normal_values(key_list[4], (FILTERS, 3, 3), 9 ** -0.5, 2.0),
        "conv_bias": normal_values(key_list[5], (FILTERS,), 0.3, 3.0, (), jnp.float32),
        "fc_weight": normal_values(key_list[6], (FLAT, D), FLAT ** -0.5, 0.0625),
        "fc_bias": normal_values(key_list[7], (D,), 0.3, 3.0, (), jnp.float32),
        "head_ids": set_ends(ranked_ids(key_list[8], (ROUNDS, TRI_ALL), ENT_DEV, 2), jax.random.fold_in(key_list[8], 3), 0, ENT_DEV - 1).astype(jnp.int32),
        "rel_ids": set_ends(ranked_ids(key_list[9], (ROUNDS, TRI_ALL), REL, 2), jax.random.fold_in(key_list[9], 3), 0, REL - 1).astype(jnp.int32),
        "tail_ids": set_ends(jax.random.randint(key_list[10], (ROUNDS, TRI_ALL), 0, ENT_DEV), jax.random.fold_in(key_list[10], 1), 0, ENT_DEV - 1).astype(jnp.int32),
        "neg_ids": set_ends(jax.random.randint(key_list[11], (ROUNDS, NEG_ALL), 0, ENT_DEV), jax.random.fold_in(key_list[11], 1), 0, ENT_DEV - 1).astype(jnp.int32),
    }


negative_weight = 0.03125
learn_rate = 0.5

def silu_slope(values):
    sigma = jax.nn.sigmoid(values)
    return sigma * (1.0 + values * (1.0 - sigma))

def conv_forward(picture, conv_weight, conv_bias):
    height = picture.shape[0] - 2
    across = picture.shape[1] - 2
    patches = jnp.stack([picture[row_off:row_off + height, col_off:col_off + across] for row_off in range(3) for col_off in range(3)])
    filters = conv_weight.reshape(FILTERS, 9).astype(jnp.float32)
    result = jnp.einsum('fk,kijt->fijt', filters, patches.astype(jnp.float32))
    return result + conv_bias[:, None, None, None]

def conv_backward(pre1_grad, conv_weight):
    filters = conv_weight.reshape(FILTERS, 9).astype(jnp.float32)
    spread = jnp.einsum('fk,fijt->kijt', filters, pre1_grad.astype(jnp.float32))
    height = spread.shape[1]
    across = spread.shape[2]
    total = jnp.zeros((height + 2, across + 2, spread.shape[3]), jnp.float32)
    for offset in range(9):
        row_off, col_off = divmod(offset, 3)
        total = total.at[row_off:row_off + height, col_off:col_off + across].add(spread[offset])
    return total

def block_pass(head_rows, rel_rows, tail_rows, negset, conv_weight, conv_bias, fc_weight, fc_bias):
    number = head_rows.shape[0]
    picture = jnp.concatenate([head_rows.reshape(number, EMB_H, EMB_W), rel_rows.reshape(number, EMB_H, EMB_W)], axis=1)
    picture = jnp.transpose(picture, (1, 2, 0))
    pre1 = conv_forward(picture, conv_weight, conv_bias)
    act = jax.nn.silu(pre1).astype(jnp.bfloat16).reshape(FLAT, number)
    pre2 = jnp.dot(fc_weight.T, act, preferred_element_type=jnp.float32) + fc_bias[:, None]
    query = jax.nn.silu(pre2).astype(jnp.bfloat16)
    tail_cols = tail_rows.T.astype(jnp.float32)
    pos_score = lax.optimization_barrier(jnp.sum(query.astype(jnp.float32) * tail_cols, axis=0))
    neg_score = jnp.dot(negset, query, preferred_element_type=jnp.float32)
    pos_grad = -jax.nn.sigmoid(-pos_score)
    neg_grad = (negative_weight * jax.nn.sigmoid(neg_score)).astype(jnp.bfloat16)
    query_grad = pos_grad[None, :] * tail_cols + lax.dot_general(negset, neg_grad, (((0,), (0,)), ((), ())), preferred_element_type=jnp.float32)
    pre2_grad = (query_grad * silu_slope(pre2)).astype(jnp.bfloat16)
    act_grad = jnp.dot(fc_weight, pre2_grad, preferred_element_type=jnp.float32)
    pre1_grad = (act_grad.reshape(pre1.shape) * silu_slope(pre1)).astype(jnp.bfloat16)
    picture_grad = conv_backward(pre1_grad, conv_weight)
    head_grad = jnp.transpose(picture_grad[:EMB_H], (2, 0, 1)).reshape(number, D)
    relation_grad = jnp.transpose(picture_grad[EMB_H:], (2, 0, 1)).reshape(number, D)
    tail_grad = (pos_grad[None, :] * query.astype(jnp.float32)).T
    negset_grad = lax.dot_general(neg_grad, query, (((1,), (1,)), ((), ())), preferred_element_type=jnp.float32)
    return (head_grad, relation_grad, tail_grad, negset_grad)

def adagrad(rows, state, gradient):
    state = state + lax.optimization_barrier(jnp.mean(gradient * gradient, axis=1))
    rows = rows - learn_rate * gradient / jnp.sqrt(state)[:, None]
    return (rows, state)

def reference(entity_rows, entity_state, relation_rows, relation_state, conv_weight, conv_bias, fc_weight, fc_bias, head_ids, rel_ids, tail_ids, neg_ids):
    blocks = N_GROUP * N_SHARD
    pick_rows = jax.vmap(jax.vmap(lambda table_rows, row_index: table_rows[row_index]))
    for round_index in range(ROUNDS):
        partner_bit = 1 << round_index
        partner_group = np.arange(N_GROUP) ^ partner_bit
        ent_bf = entity_rows.astype(jnp.bfloat16).reshape(N_GROUP, N_SHARD, ENT_DEV, D)
        rel_bf = relation_rows.astype(jnp.bfloat16)
        partner = ent_bf[partner_group]
        heads = head_ids[round_index].reshape(N_GROUP, N_SHARD, TRI_DEV)
        tails = tail_ids[round_index].reshape(N_GROUP, N_SHARD, TRI_DEV)
        negatives = neg_ids[round_index].reshape(N_GROUP, N_SHARD, NEG_DEV)
        head_rows = pick_rows(ent_bf, heads).reshape(blocks, TRI_DEV, D)
        tail_rows = pick_rows(partner, tails).reshape(blocks, TRI_DEV, D)
        rel_rows = rel_bf[rel_ids[round_index]].reshape(blocks, TRI_DEV, D)
        negset = pick_rows(partner, negatives).reshape(N_GROUP, NEG_SPAN, D)
        negset_each = jnp.repeat(negset, N_SHARD, axis=0)

        def per_block(inputs):
            return block_pass(inputs[0], inputs[1], inputs[2], inputs[3], conv_weight, conv_bias, fc_weight, fc_bias)
        head_grad, relation_grad, tail_grad, negset_grad = lax.map(per_block, (head_rows, rel_rows, tail_rows, negset_each))
        negset_sum = negset_grad.reshape(N_GROUP, N_SHARD, NEG_SPAN, D).sum(axis=1).reshape(N_GROUP * N_SHARD * NEG_DEV, D)
        own_base = (jnp.arange(blocks, dtype=jnp.int32) * ENT_DEV).reshape(N_GROUP, N_SHARD, 1)
        partner_base = ((jnp.asarray(partner_group, dtype=jnp.int32)[:, None] * N_SHARD + jnp.arange(N_SHARD, dtype=jnp.int32)[None, :]) * ENT_DEV)[:, :, None]
        head_index = (own_base + heads).reshape(-1)
        tail_index = (partner_base + tails).reshape(-1)
        neg_index = (partner_base + negatives).reshape(-1)
        entity_grad = jnp.zeros((ENTITIES, D), jnp.float32)
        entity_grad = entity_grad.at[head_index].add(head_grad.reshape(-1, D))
        entity_grad = entity_grad.at[tail_index].add(tail_grad.reshape(-1, D))
        entity_grad = entity_grad.at[neg_index].add(negset_sum)
        rel_total = jnp.zeros((REL, D), jnp.float32).at[rel_ids[round_index]].add(relation_grad.reshape(-1, D))
        entity_rows, entity_state = adagrad(entity_rows, entity_state, entity_grad)
        relation_rows, relation_state = adagrad(relation_rows, relation_state, rel_total)
    return (entity_rows, entity_state, relation_rows, relation_state)
```

```python
import functools

import jax
import jax.numpy as jnp
import numpy as np
from jax import lax
from jax.experimental import pallas as pl
from jax.experimental.pallas import tpu as pltpu
from jax.sharding import PartitionSpec as P

D = 200
FILTERS = 32
FLAT = 10368
REL = 1387
REL_PAD = 1536
BLK = 48
TRI = 128
NEG = 32
ENT = 1024
CHUNK = 1152
STEPS = FLAT // CHUNK
MESH = pl.DeviceIdType.MESH
F32 = jnp.float32
BF16 = jnp.bfloat16

negative_weight = 0.03125
learn_rate = 0.5

NT = (((1,), (1,)), ((), ()))


def nn(a, b):
    return jnp.dot(a, b, preferred_element_type=F32)


def nt(a, b):
    return lax.dot_general(a, b, NT, preferred_element_type=F32)


def spread_dot(one_hot, values):
    high = values.astype(BF16)
    low = (values - high.astype(F32)).astype(BF16)
    return nn(one_hot, high) + nn(one_hot, low)


def hot_cols(ids_col, extent):
    where = lax.broadcasted_iota(jnp.int32, (ids_col.shape[0], extent), 1)
    return jnp.where(where == ids_col, 1.0, 0.0).astype(BF16)


def hot_rows(ids_row, extent):
    where = lax.broadcasted_iota(jnp.int32, (extent, ids_row.shape[1]), 0)
    return jnp.where(where == ids_row, 1.0, 0.0).astype(BF16)


def toeplitz_kernel(place_ref, wb_ref, t_ref, bias_ref):
    base = place_ref[0:1, :]
    filt = place_ref[1:2, :]
    own = jnp.where(
        lax.broadcasted_iota(jnp.int32, (FILTERS, CHUNK), 0) == filt, 1.0, 0.0
    ).astype(F32)
    wide = jnp.dot(wb_ref[...], own, precision=lax.Precision.HIGHEST, preferred_element_type=F32)
    bias_ref[...] = wide[9:10, :]
    for half in range(2):

        def tile(step, carry):
            first = pl.multiple_of(step * 16, 16)
            apart = lax.broadcasted_iota(jnp.int32, (16, CHUNK), 0) + (first + 200 * half) - base
            out = jnp.zeros((16, CHUNK), F32)
            for k in range(9):
                a, c = divmod(k, 3)
                out = jnp.where(apart == a * 20 + c, wide[k : k + 1, :], out)
            t_ref[half, pl.ds(first, 16), :] = out.astype(BF16)
            return carry

        lax.fori_loop(0, 13, tile, 0)


def toeplitz(conv_weight, conv_bias):
    q = np.arange(FLAT)
    rest = q % 324
    place = np.zeros((8, FLAT), np.int32)
    place[0] = (rest // 18) * 20 + rest % 18
    place[1] = q // 324
    wb = jnp.concatenate(
        [
            conv_weight.reshape(FILTERS, 9).astype(F32),
            conv_bias[:, None],
            jnp.zeros((FILTERS, 6), F32),
        ],
        axis=1,
    ).T
    return pl.pallas_call(
        toeplitz_kernel,
        grid=(STEPS,),
        out_shape=(
            jax.ShapeDtypeStruct((2, 208, FLAT), BF16),
            jax.ShapeDtypeStruct((1, FLAT), F32),
        ),
        in_specs=[
            pl.BlockSpec((8, CHUNK), lambda j: (0, j)),
            pl.BlockSpec((16, FILTERS), lambda j: (0, 0)),
        ],
        out_specs=(
            pl.BlockSpec((2, 208, CHUNK), lambda j: (0, 0, j)),
            pl.BlockSpec((1, CHUNK), lambda j: (0, j)),
        ),
        name="toeplitz",
    )(jnp.asarray(place), wb)


def pass_kernel(
    cols_ref, rows_ref, ent_ref, rel_ref, t_ref, w_ref, bias_ref, fc_bias_ref, tail_ref, neg_ref,
    head_out, rel_out, neg_out, tail_out,
    pic_h, pic_r, slope, acc, grad_h, grad_r, pre2_grad,
):
    phase = pl.program_id(0)
    step = pl.program_id(1)

    @pl.when((phase == 0) & (step == 0))
    def _():
        pic_h[...] = nn(hot_cols(cols_ref[:, 0:1], ENT), ent_ref[...].astype(BF16)).astype(BF16)
        pic_r[...] = nn(hot_cols(cols_ref[:, 1:2], REL), rel_ref[...].astype(BF16)).astype(BF16)
        acc[...] = jnp.zeros_like(acc)
        grad_h[...] = jnp.zeros_like(grad_h)
        grad_r[...] = jnp.zeros_like(grad_r)

    @pl.when(phase == 0)
    def _():
        pre1 = (
            nn(pic_h[...], t_ref[0, :D, :]) + nn(pic_r[...], t_ref[1, :D, :]) + bias_ref[...]
        )
        sigma = 0.5 * jnp.tanh(0.5 * pre1) + 0.5
        act = pre1 * sigma
        slope[step] = sigma + act * (1.0 - sigma)
        acc[...] += nn(act.astype(BF16), w_ref[...])

    @pl.when((phase == 0) & (step == STEPS - 1))
    def _():
        pre2 = acc[...] + fc_bias_ref[...]
        sigma = jax.nn.sigmoid(pre2)
        query = (pre2 * sigma).astype(BF16)
        tails = tail_ref[...].astype(F32)
        wide = query.astype(F32)
        pos_grad = -jax.nn.sigmoid(-jnp.sum(wide * tails, axis=1, keepdims=True))
        negset = neg_ref[...]
        by_row = (negative_weight * jax.nn.sigmoid(nt(query, negset))).astype(BF16)
        by_neg = (negative_weight * jax.nn.sigmoid(nt(negset, query))).astype(BF16)
        query_grad = pos_grad * tails + nn(by_row, negset)
        pre2_grad[...] = (query_grad * (sigma * (1.0 + pre2 * (1.0 - sigma)))).astype(BF16)
        neg_out[...] = nn(by_neg, query)
        tail_out[...] = pos_grad * wide

    @pl.when(phase == 1)
    def _():
        act_grad = nt(pre2_grad[...], w_ref[...])
        pre1_grad = (act_grad * slope[step]).astype(BF16)
        grad_h[...] += nt(pre1_grad, t_ref[0, :D, :])
        grad_r[...] += nt(pre1_grad, t_ref[1, :D, :])

    @pl.when((phase == 1) & (step == STEPS - 1))
    def _():
        head_out[...] = spread_dot(hot_rows(rows_ref[0:1, :], ENT), grad_h[...])
        rel_out[...] = spread_dot(hot_rows(rows_ref[1:2, :], REL_PAD), grad_r[...])


def block_pass(cols, rows, ent, rel, t_mat, fc_weight, bias, fc_bias, tails, negset):
    whole = lambda *shape: pl.BlockSpec(shape, lambda p, j: (0,) * len(shape))
    return pl.pallas_call(
        pass_kernel,
        grid=(2, STEPS),
        out_shape=(
            jax.ShapeDtypeStruct((ENT, D), F32),
            jax.ShapeDtypeStruct((REL_PAD, D), F32),
            jax.ShapeDtypeStruct((1024, D), F32),
            jax.ShapeDtypeStruct((TRI, D), F32),
        ),
        in_specs=[
            whole(TRI, 2),
            whole(2, TRI),
            whole(ENT, D),
            whole(REL, D),
            pl.BlockSpec((2, 208, CHUNK), lambda p, j: (0, 0, j)),
            pl.BlockSpec((CHUNK, D), lambda p, j: (j, 0)),
            pl.BlockSpec((1, CHUNK), lambda p, j: (0, j)),
            whole(1, D),
            whole(TRI, D),
            whole(1024, D),
        ],
        out_specs=(whole(ENT, D), whole(REL_PAD, D), whole(1024, D), whole(TRI, D)),
        scratch_shapes=[
            pltpu.VMEM((TRI, D), BF16),
            pltpu.VMEM((TRI, D), BF16),
            pltpu.VMEM((STEPS, TRI, CHUNK), F32),
            pltpu.VMEM((TRI, D), F32),
            pltpu.VMEM((TRI, D), F32),
            pltpu.VMEM((TRI, D), F32),
            pltpu.VMEM((TRI, D), BF16),
        ],
        compiler_params=pltpu.CompilerParams(vmem_limit_bytes=56 << 20),
        name="block_pass",
    )(cols, rows, ent, rel, t_mat, fc_weight, bias, fc_bias, tails, negset)


class Place:
    def __init__(self):
        group = lax.axis_index("group")
        shard = lax.axis_index("shard")
        self.x = group % 4
        self.y_hi = group // 4
        self.y_lo = shard // 16
        self.z = (shard // 2) % 8
        self.core = shard % 2
        self.y = self.y_hi * 2 + self.y_lo

    def at(self, x=None, y=None, z=None, core=None):
        x = self.x if x is None else x
        y = self.y if y is None else y
        z = self.z if z is None else z
        core = self.core if core is None else core
        return ((y // 2) * 4 + x, (y % 2) * 16 + z * 2 + core)

    def mate(self):
        return self.at(core=1 - self.core)

    def beside(self):
        return self.at(y=self.y_hi * 2 + 1 - self.y_lo)

    def partner(self, bit):
        if bit == 0:
            return self.at(x=self.x + 1 - 2 * (self.x % 2))
        return self.at(x=(self.x + 2) % 4)


class Copies:
    def __init__(self, send, recv):
        self.send, self.recv, self.used = send, recv, 0

    def start(self, src, dst, device):
        copy = pltpu.make_async_remote_copy(
            src_ref=src,
            dst_ref=dst,
            send_sem=self.send.at[self.used],
            recv_sem=self.recv.at[self.used],
            device_id=device,
            device_id_type=MESH,
        )
        self.used += 1
        copy.start()
        return copy


def greet(peers):
    barrier = pltpu.get_barrier_semaphore()
    for peer in peers:
        pl.semaphore_signal(barrier, inc=1, device_id=peer, device_id_type=MESH)
    pl.semaphore_wait(barrier, len(peers))


def wait_all(copies):
    for copy in copies:
        copy.wait()


def pick_rows(cols_ref, table_bf, pick_tail, pick_neg):
    pick_tail[...] = nn(hot_cols(cols_ref[0:TRI, :], ENT), table_bf).astype(BF16)
    pick_neg[...] = nn(hot_cols(cols_ref[TRI : TRI + NEG, :], ENT), table_bf).astype(BF16)


def rows_kernel(bit, cols_ref, ent_ref, tail_out, neg_out, pick_tail, pick_neg, tails, negs, send, recv):
    me = Place()
    copies = Copies(send, recv)
    pick_rows(cols_ref, ent_ref[...].astype(BF16), pick_tail, pick_neg)
    z_peers = [me.at(z=(me.z + d) % 8) for d in range(1, 8)]
    greet([me.mate(), me.beside(), me.partner(bit)] + z_peers)
    own = negs.at[me.core, me.y_lo, me.z]
    first = copies.start(pick_neg, own, me.partner(bit))
    tail = copies.start(pick_tail, tails, me.partner(bit))
    first.wait()
    wait_all([copies.start(own, own, peer) for peer in z_peers])
    half = negs.at[me.core, me.y_lo]
    copies.start(half, half, me.beside()).wait()
    half = negs.at[me.core]
    copies.start(half, half, me.mate()).wait()
    tail.wait()
    tail_out[...] = tails[...]
    neg_out[...] = negs[...]


VMEM_SPEC = pl.BlockSpec(memory_space=pltpu.VMEM)


def fetch_rows(bit, cols, ent):
    number = 11
    return pl.pallas_call(
        functools.partial(rows_kernel, bit),
        out_shape=(
            jax.ShapeDtypeStruct((TRI, D), BF16),
            jax.ShapeDtypeStruct((2, 2, 8, NEG, D), BF16),
        ),
        in_specs=[VMEM_SPEC] * 2,
        out_specs=(VMEM_SPEC, VMEM_SPEC),
        scratch_shapes=[
            pltpu.VMEM((TRI, D), BF16),
            pltpu.VMEM((NEG, D), BF16),
            pltpu.VMEM((TRI, D), BF16),
            pltpu.VMEM((2, 2, 8, NEG, D), BF16),
            pltpu.SemaphoreType.DMA((number,)),
            pltpu.SemaphoreType.DMA((number,)),
        ],
        compiler_params=pltpu.CompilerParams(collective_id=0, has_side_effects=True),
        name="fetch_rows",
    )(cols, ent)


def step_of(rows, state, gradient):
    state = state + jnp.sum(gradient * gradient, axis=1, keepdims=True) * (1.0 / D)
    return rows - learn_rate * gradient * lax.rsqrt(state), state


def update_kernel(
    bit, more,
    rel_part, neg_part, tail_grad, head_sum, ent, ent_state, rel, rel_state, rows_ref, *rest,
):
    if more:
        (cols_ref, ent_out, ent_state_out, rel_out, rel_state_out, tail_out, neg_out), rest = rest[:7], rest[7:]
    else:
        (ent_out, ent_state_out, rel_out, rel_state_out), rest = rest[:4], rest[4:]
    (r0, s1_send, s1_recv, acc1, s2_recv, z_buf, g_buf,
     b1, b2_send, b2_recv, b3_send, b3_recv, b4_send, b4_recv, tail_in), rest = rest[:15], rest[15:]
    if more:
        (pick_tail, pick_neg, tails, negs), rest = rest[:4], rest[4:]
    send, recv = rest
    me = Place()
    copies = Copies(send, recv)
    c, z, y_lo = me.core, me.z, me.y_lo
    first = me.x * (1 - c) + me.y * c
    second = me.y * (1 - c) + me.x * c

    def along_first(i):
        return me.at(x=i * (1 - c) + me.x * c, y=i * c + me.y * (1 - c))

    def along_second(i):
        return me.at(x=me.x * (1 - c) + i * c, y=i * (1 - c) + me.y * c)

    firsts = [(first + d) % 4 for d in range(1, 4)]
    seconds = [(second + d) % 4 for d in range(1, 4)]
    zs = [(z + d) % 8 for d in range(1, 8)]
    mate, partner = me.mate(), me.partner(bit)
    greet(
        [mate]
        + [along_first(i) for i in firsts]
        + [along_second(i) for i in seconds]
        + [me.at(z=i) for i in zs]
    )
    b1_copy = copies.start(neg_part.at[1 - c], b1, mate)
    s0_copy = copies.start(rel_part.at[1 - c], r0, mate)
    tail_copy = copies.start(tail_grad, tail_in, partner)
    b1_copy.wait()
    b2_send[...] = (neg_part[c, 1 - y_lo] + b1[1 - y_lo]).astype(BF16)
    b2_copy = copies.start(b2_send, b2_recv, me.beside())
    s0_copy.wait()
    for i in range(4):
        s1_send[i] = (rel_part[c, i] + r0[i]).astype(BF16)
    s1_copies = [
        copies.start(s1_send.at[i], s1_recv.at[d], along_first(i)) for d, i in enumerate(firsts)
    ]
    b2_copy.wait()
    b3_send[...] = (neg_part[c, y_lo] + b1[y_lo] + b2_recv[...].astype(F32)).astype(BF16)
    b3_copies = [
        copies.start(b3_send.at[i], b3_recv.at[d], me.at(z=i)) for d, i in enumerate(zs)
    ]
    wait_all(s1_copies)
    acc1[...] = (
        rel_part[c, first]
        + r0[first]
        + s1_recv[0].astype(F32)
        + s1_recv[1].astype(F32)
        + s1_recv[2].astype(F32)
    )
    s2_copies = [
        copies.start(acc1.at[i], s2_recv.at[d], along_second(i)) for d, i in enumerate(seconds)
    ]
    wait_all(s2_copies)
    z_buf[z] = (acc1[second] + s2_recv[0] + s2_recv[1] + s2_recv[2]).astype(BF16)
    z_copies = [copies.start(z_buf.at[z], z_buf.at[z], me.at(z=i)) for i in zs]
    wait_all(b3_copies)
    share = b3_send[z].astype(F32)
    for d in range(7):
        share = share + b3_recv[d].astype(F32)
    b4_send[...] = share
    b4_copy = copies.start(b4_send, b4_recv, partner)
    wait_all(z_copies)
    total = z_buf[0].astype(F32)
    for i in range(1, 8):
        total = total + z_buf[i].astype(F32)
    g_buf[c, first, second] = total.astype(BF16)
    own = g_buf.at[c, first, second]
    s4_copies = [copies.start(own, own, along_second(i)) for i in seconds]
    b4_copy.wait()
    tail_copy.wait()
    gradient = (
        head_sum[...]
        + spread_dot(hot_rows(rows_ref[0:1, 0:TRI], ENT), tail_in[...])
        + spread_dot(hot_rows(rows_ref[0:1, TRI : TRI + NEG], ENT), b4_recv[...])
    )
    new_rows, new_state = step_of(ent[...], ent_state[...], gradient)
    ent_out[...] = new_rows
    ent_state_out[...] = new_state
    if more:
        pick_rows(cols_ref, new_rows.astype(BF16), pick_tail, pick_neg)
        following = me.partner(1 - bit)
        mine = negs.at[c, y_lo, z]
        a1_copy = copies.start(pick_neg, mine, following)
        a0_copy = copies.start(pick_tail, tails, following)
    wait_all(s4_copies)
    own = g_buf.at[c, first]
    s5_copies = [copies.start(own, own, along_first(i)) for i in firsts]
    if more:
        a1_copy.wait()
        a2_copies = [copies.start(mine, mine, me.at(z=i)) for i in zs]
    wait_all(s5_copies)
    own = g_buf.at[c]
    s6_copy = copies.start(own, own, mate)
    if more:
        wait_all(a2_copies)
        half = negs.at[c, y_lo]
        a3_copy = copies.start(half, half, me.beside())
    s6_copy.wait()
    for k in range(29):
        low, high = k * BLK, min(k * BLK + BLK, REL)
        g = g_buf[k // 16, (k // 4) % 4, k % 4].astype(F32)[: high - low]
        new_rows, new_state = step_of(rel[low:high, :], rel_state[low:high, :], g)
        rel_out[low:high, :] = new_rows
        rel_state_out[low:high, :] = new_state
    if more:
        a3_copy.wait()
        half = negs.at[c]
        copies.start(half, half, mate).wait()
        a0_copy.wait()
        tail_out[...] = tails[...]
        neg_out[...] = negs[...]


def update(bit, more, rel_part, neg_part, tail_grad, head_sum, ent, ent_state, rel, rel_state, rows, cols):
    out_shape = [
        jax.ShapeDtypeStruct((ENT, D), F32),
        jax.ShapeDtypeStruct((ENT, 1), F32),
        jax.ShapeDtypeStruct((REL, D), F32),
        jax.ShapeDtypeStruct((REL, 1), F32),
    ]
    scratch = [
        pltpu.VMEM((4, 4, BLK, D), F32),
        pltpu.VMEM((4, 4, BLK, D), BF16),
        pltpu.VMEM((3, 4, BLK, D), BF16),
        pltpu.VMEM((4, BLK, D), F32),
        pltpu.VMEM((3, BLK, D), F32),
        pltpu.VMEM((8, BLK, D), BF16),
        pltpu.VMEM((2, 4, 4, BLK, D), BF16),
        pltpu.VMEM((2, 8, NEG, D), F32),
        pltpu.VMEM((8, NEG, D), BF16),
        pltpu.VMEM((8, NEG, D), BF16),
        pltpu.VMEM((8, NEG, D), BF16),
        pltpu.VMEM((7, NEG, D), BF16),
        pltpu.VMEM((NEG, D), F32),
        pltpu.VMEM((NEG, D), F32),
        pltpu.VMEM((TRI, D), F32),
    ]
    operands = [
        rel_part.reshape(2, 4, 4, BLK, D),
        neg_part.reshape(2, 2, 8, NEG, D),
        tail_grad, head_sum, ent, ent_state, rel, rel_state, rows,
    ]
    number = 1 + 1 + 1 + 1 + 3 + 7 + 3 + 7 + 1 + 3 + 3 + 1
    if more:
        number += 2 + 7 + 1 + 1
        operands.append(cols)
        out_shape += [
            jax.ShapeDtypeStruct((TRI, D), BF16),
            jax.ShapeDtypeStruct((2, 2, 8, NEG, D), BF16),
        ]
        scratch += [
            pltpu.VMEM((TRI, D), BF16),
            pltpu.VMEM((NEG, D), BF16),
            pltpu.VMEM((TRI, D), BF16),
            pltpu.VMEM((2, 2, 8, NEG, D), BF16),
        ]
    scratch += [pltpu.SemaphoreType.DMA((number,)), pltpu.SemaphoreType.DMA((number,))]
    return pl.pallas_call(
        functools.partial(update_kernel, bit, more),
        out_shape=tuple(out_shape),
        in_specs=[VMEM_SPEC] * len(operands),
        out_specs=tuple([VMEM_SPEC] * len(out_shape)),
        scratch_shapes=scratch,
        compiler_params=pltpu.CompilerParams(
            collective_id=1 + bit, has_side_effects=True, vmem_limit_bytes=56 << 20
        ),
        name="update",
    )(*operands)


def partner_ids(ids, bit):
    route = [(i, i ^ (1 << bit)) for i in range(8)]
    return lax.ppermute(ids, "group", route)


def shards(
    entity_rows, entity_state, relation_rows, relation_state,
    conv_weight, conv_bias, fc_weight, fc_bias,
    head_ids, rel_ids, tail_ids, neg_ids,
):
    asked = jnp.concatenate([tail_ids, neg_ids], axis=1)
    asked = [partner_ids(asked[r : r + 1], r) for r in range(2)]
    t_mat, bias = toeplitz(conv_weight, conv_bias)
    own_rows = [jnp.stack([head_ids[r], rel_ids[r]]) for r in range(2)]
    own_cols = [ids.T for ids in own_rows]
    asked_cols = [ids.reshape(TRI + NEG, 1) for ids in asked]
    ent, ent_state = entity_rows, entity_state.reshape(ENT, 1)
    rel, rel_state = relation_rows, relation_state.reshape(REL, 1)
    tails, negset = fetch_rows(0, asked_cols[0], ent)
    for r in range(2):
        head_sum, rel_part, neg_part, tail_grad = block_pass(
            own_cols[r], own_rows[r], ent, rel, t_mat, fc_weight, bias, fc_bias.reshape(1, D),
            tails, negset.reshape(1024, D),
        )
        out = update(
            r, r == 0, rel_part, neg_part, tail_grad, head_sum,
            ent, ent_state, rel, rel_state, asked[r], asked_cols[1],
        )
        ent, ent_state, rel, rel_state = out[:4]
        if r == 0:
            tails, negset = out[4:]
    return ent, ent_state.reshape(ENT), rel, rel_state.reshape(REL)


def solution(mesh):
    both = ("group", "shard")
    in_specs = (
        P(both, None), P(both), P(), P(), P(), P(), P(), P(),
        P(None, both), P(None, both), P(None, both), P(None, both),
    )
    out_specs = (P(both, None), P(both), P(), P())
    return jax.shard_map(shards, mesh=mesh, in_specs=in_specs, out_specs=out_specs, check_vma=False)
```

```python
import functools

import jax
import jax.numpy as jnp
import numpy as np
from jax import lax
from jax.experimental import pallas as pl
from jax.experimental.pallas import tpu as pltpu
from jax.sharding import PartitionSpec as P

D = 200
FILTERS = 32
FLAT = 10368
REL = 1387
REL_PAD = 1536
BLK = 48
TRI = 128
NEG = 32
ENT = 1024
CHUNK = 1152
STEPS = FLAT // CHUNK
WIDE = 240
MESH = pl.DeviceIdType.MESH
F32 = jnp.float32
BF16 = jnp.bfloat16

negative_weight = 0.03125
learn_rate = 0.5

NT = (((1,), (1,)), ((), ()))


def nn(a, b):
    return jnp.dot(a, b, preferred_element_type=F32)


def nt(a, b):
    return lax.dot_general(a, b, NT, preferred_element_type=F32)


def spread_dot(one_hot, values):
    high = values.astype(BF16)
    low = (values - high.astype(F32)).astype(BF16)
    return nn(one_hot, high) + nn(one_hot, low)


def hot_rows(ids_row, extent):
    where = lax.broadcasted_iota(jnp.int32, (extent, ids_row.shape[1]), 0)
    return jnp.where(where == ids_row, 1.0, 0.0).astype(BF16)


def spacing():
    d = np.arange(D)
    out = np.zeros((D, WIDE), np.float32)
    out[d, d // 20 * 24 + d % 20] = 1.0
    return jnp.asarray(out, BF16)


def spread_nt(one_hot, values):
    high = values.astype(BF16)
    low = (values - high.astype(F32)).astype(BF16)
    return nt(one_hot, high) + nt(one_hot, low)


def spread_nt_right(values, one_hot):
    high = values.astype(BF16)
    low = (values - high.astype(F32)).astype(BF16)
    return nt(high, one_hot) + nt(low, one_hot)


def pass_kernel(
    round_index,
    head_ids, rel_ids, ent_ref, rel_ref, t_hbm, w_hbm, bias_ref, fc_bias_ref, tail_ref, neg_ref, space_ref,
    head_out, rel_out, neg_out, tail_out,
    t_all, w_all, pic_h, pic_r, slope, acc, grad_h, grad_r, pre2_grad, t_sem, w_sem,
):
    phase = pl.program_id(0)
    step = pl.program_id(1)

    def fetch(j):
        return (
            pltpu.make_async_copy(t_hbm.at[j], t_all.at[j], t_sem.at[j]),
            pltpu.make_async_copy(
                w_hbm.at[:, pl.ds(pl.multiple_of(j * CHUNK, CHUNK), CHUNK)], w_all.at[j], w_sem.at[j]
            ),
        )

    @pl.when((phase == 0) & (step == 0))
    def _():
        for j in range(STEPS):
            for copy in fetch(j):
                copy.start()
        heads = nn(ent_ref[...].astype(BF16), hot_rows(head_ids[round_index : round_index + 1, :], ENT))
        pic_h[...] = nn(heads.T.astype(BF16), space_ref[...]).astype(BF16)
        relations = nn(rel_ref[...].astype(BF16), hot_rows(rel_ids[round_index : round_index + 1, :], REL))
        pic_r[...] = nn(relations.T.astype(BF16), space_ref[...]).astype(BF16)
        acc[...] = jnp.zeros_like(acc)
        grad_h[...] = jnp.zeros_like(grad_h)
        grad_r[...] = jnp.zeros_like(grad_r)

    @pl.when(phase == 0)
    def _():
        for copy in fetch(step):
            copy.wait()
        pre1 = nn(pic_h[...], t_all[step, 0]) + nn(pic_r[...], t_all[step, 1]) + bias_ref[step]
        sigma = 0.5 * jnp.tanh(0.5 * pre1) + 0.5
        act = pre1 * sigma
        slope[step] = sigma + act * (1.0 - sigma)
        acc[...] += nt(act.astype(BF16), w_all[step])

    @pl.when((phase == 0) & (step == STEPS - 1))
    def _():
        pre2 = acc[...] + fc_bias_ref[...]
        sigma = jax.nn.sigmoid(pre2)
        query = (pre2 * sigma).astype(BF16)
        tails = tail_ref[...].astype(F32)
        wide = query.astype(F32)
        pos_grad = -jax.nn.sigmoid(-jnp.sum(wide * tails, axis=1, keepdims=True))
        negset = neg_ref[...]
        by_row = (negative_weight * jax.nn.sigmoid(nt(query, negset))).astype(BF16)
        by_neg = (negative_weight * jax.nn.sigmoid(nt(negset, query))).astype(BF16)
        query_grad = pos_grad * tails + nn(by_row, negset)
        pre2_grad[...] = (query_grad * (sigma * (1.0 + pre2 * (1.0 - sigma)))).astype(BF16)
        neg_out[...] = nn(by_neg, query).astype(BF16)
        tail_out[...] = (pos_grad * wide).T

    @pl.when(phase == 1)
    def _():
        act_grad = nn(pre2_grad[...], w_all[step])
        pre1_grad = (act_grad * slope[step]).astype(BF16)
        grad_h[...] += nt(pre1_grad, t_all[step, 0])
        grad_r[...] += nt(pre1_grad, t_all[step, 1])

    @pl.when((phase == 1) & (step == STEPS - 1))
    def _():
        head_out[...] = spread_nt(space_ref[...], grad_h[...])
        rows = spread_nt_right(grad_r[...], space_ref[...])
        rel_out[...] = spread_dot(hot_rows(rel_ids[round_index : round_index + 1, :], REL_PAD), rows).astype(BF16)


def block_pass(round_index, head_ids, rel_ids, ent, rel, t_mat, w_mat, bias, fc_bias, tails, negset):
    whole = lambda *shape: pl.BlockSpec(shape, lambda p, j: (0,) * len(shape))
    anywhere = pl.BlockSpec(memory_space=pl.ANY)
    return pl.pallas_call(
        functools.partial(pass_kernel, round_index),
        grid=(2, STEPS),
        out_shape=(
            jax.ShapeDtypeStruct((D, TRI), F32),
            jax.ShapeDtypeStruct((REL_PAD, D), BF16),
            jax.ShapeDtypeStruct((1024, D), BF16),
            jax.ShapeDtypeStruct((D, TRI), F32),
        ),
        in_specs=[
            whole(2, TRI),
            whole(2, TRI),
            whole(D, ENT),
            whole(D, REL),
            anywhere,
            anywhere,
            whole(STEPS, 1, CHUNK),
            whole(1, D),
            whole(TRI, D),
            whole(1024, D),
            whole(D, WIDE),
        ],
        out_specs=(whole(D, TRI), whole(REL_PAD, D), whole(1024, D), whole(D, TRI)),
        scratch_shapes=[
            pltpu.VMEM((STEPS, 2, WIDE, CHUNK), BF16),
            pltpu.VMEM((STEPS, D, CHUNK), BF16),
            pltpu.VMEM((TRI, WIDE), BF16),
            pltpu.VMEM((TRI, WIDE), BF16),
            pltpu.VMEM((STEPS, TRI, CHUNK), F32),
            pltpu.VMEM((TRI, D), F32),
            pltpu.VMEM((TRI, WIDE), F32),
            pltpu.VMEM((TRI, WIDE), F32),
            pltpu.VMEM((TRI, D), BF16),
            pltpu.SemaphoreType.DMA((STEPS,)),
            pltpu.SemaphoreType.DMA((STEPS,)),
        ],
        compiler_params=pltpu.CompilerParams(vmem_limit_bytes=56 << 20),
        name="block_pass",
    )(head_ids, rel_ids, ent, rel, t_mat, w_mat, bias, fc_bias, tails, negset, spacing())


class Place:
    def __init__(self):
        group = lax.axis_index("group")
        shard = lax.axis_index("shard")
        self.x = group % 4
        self.y_hi = group // 4
        self.y_lo = shard // 16
        self.z = (shard // 2) % 8
        self.core = shard % 2
        self.y = self.y_hi * 2 + self.y_lo

    def at(self, x=None, y=None, z=None, core=None):
        x = self.x if x is None else x
        y = self.y if y is None else y
        z = self.z if z is None else z
        core = self.core if core is None else core
        return ((y // 2) * 4 + x, (y % 2) * 16 + z * 2 + core)

    def mate(self):
        return self.at(core=1 - self.core)

    def beside(self):
        return self.at(y=self.y_hi * 2 + 1 - self.y_lo)

    def partner(self, bit):
        if bit == 0:
            return self.at(x=self.x + 1 - 2 * (self.x % 2))
        return self.at(x=(self.x + 2) % 4)


class Copies:
    def __init__(self, send, recv):
        self.send, self.recv, self.used = send, recv, 0

    def start(self, src, dst, device):
        copy = pltpu.make_async_remote_copy(
            src_ref=src,
            dst_ref=dst,
            send_sem=self.send.at[self.used],
            recv_sem=self.recv.at[self.used],
            device_id=device,
            device_id_type=MESH,
        )
        self.used += 1
        copy.start()
        return copy


def greet(peers):
    barrier = pltpu.get_barrier_semaphore()
    for peer in peers:
        pl.semaphore_signal(barrier, inc=1, device_id=peer, device_id_type=MESH)
    pl.semaphore_wait(barrier, len(peers))


def wait_all(copies):
    for copy in copies:
        copy.wait()


def pick_rows(tail_ids, neg_ids, table_bf, pick_tail, pick_neg):
    pick_tail[...] = nn(table_bf, hot_rows(tail_ids, ENT)).T.astype(BF16)
    pick_neg[...] = nn(table_bf, hot_rows(neg_ids, ENT)).T.astype(BF16)


def toeplitz_chunk(j, place_ref, wb_ref, columns, t_all, bias_out):
    lanes = slice(j * CHUNK, (j + 1) * CHUNK)
    down, across, filt = (place_ref[k : k + 1, lanes] for k in range(3))
    own = jnp.where(
        lax.broadcasted_iota(jnp.int32, (FILTERS, CHUNK), 0) == filt, 1.0, 0.0
    ).astype(F32)
    wide = jnp.dot(wb_ref[...], own, precision=lax.Precision.HIGHEST, preferred_element_type=F32)
    bias_out[j] = wide[9:10, :]
    apart = lax.broadcasted_iota(jnp.int32, (24, CHUNK), 0) - across
    for a in range(3):
        out = jnp.zeros((24, CHUNK), F32)
        for c in range(3):
            out = jnp.where(apart == c, wide[3 * a + c : 3 * a + c + 1, :], out)
        columns[a] = out
    for half in range(2):

        def pair(p, carry):
            rows = []
            for one in range(2):
                away = (10 * half + 2 * p + one) - down
                out = jnp.where(away == 2, columns[2], 0.0)
                out = jnp.where(away == 1, columns[1], out)
                rows.append(jnp.where(away == 0, columns[0], out))
            first = pl.multiple_of(p * 48, 48)
            t_all[j, half, pl.ds(first, 48), :] = jnp.concatenate(rows, axis=0).astype(BF16)
            return carry

        lax.fori_loop(0, 5, pair, 0)


def rows_kernel(
    tail_ids, neg_ids, ent_ref, place_ref, wb_ref,
    tail_out, neg_out, t_out, bias_out, asked_tail, asked_neg,
    tails_in, negs_in, pick_tail, pick_neg, tails, negs, columns, t_all, t_sem, send, recv,
):
    me = Place()
    copies = Copies(send, recv)
    z_peers = [me.at(z=(me.z + d) % 8) for d in range(1, 8)]
    partners = [me.partner(0), me.partner(1)]
    greet([me.mate(), me.beside()] + partners + z_peers)
    asked = [
        (copies.start(tail_ids, tails_in.at[r], partners[r]), copies.start(neg_ids, negs_in.at[r], partners[r]))
        for r in range(2)
    ]
    out_copies = []

    def build(j):
        toeplitz_chunk(j, place_ref, wb_ref, columns, t_all, bias_out)
        copy = pltpu.make_async_copy(t_all.at[j], t_out.at[j], t_sem.at[j])
        copy.start()
        out_copies.append(copy)

    build(0)
    build(1)
    wait_all(asked[0])
    wait_all(asked[1])
    for r in range(2):
        asked_tail[r : r + 1, :] = tails_in[r, r : r + 1, :]
        asked_neg[r : r + 1, :] = negs_in[r, r : r + 1, :]
    pick_rows(tails_in[0, 0:1, :], negs_in[0, 0:1, :], ent_ref[...].astype(BF16), pick_tail, pick_neg)
    own = negs.at[me.core, me.y_lo, me.z]
    first = copies.start(pick_neg, own, partners[0])
    tail = copies.start(pick_tail, tails, partners[0])
    build(2)
    build(3)
    first.wait()
    z_copies = [copies.start(own, own, peer) for peer in z_peers]
    for j in range(4, 7):
        build(j)
    wait_all(z_copies)
    half = negs.at[me.core, me.y_lo]
    copy = copies.start(half, half, me.beside())
    for j in range(7, STEPS):
        build(j)
    copy.wait()
    half = negs.at[me.core]
    copies.start(half, half, me.mate()).wait()
    tail.wait()
    tail_out[...] = tails[...]
    neg_out[...] = negs[...]
    wait_all(out_copies)


VMEM_SPEC = pl.BlockSpec(memory_space=pltpu.VMEM)


def fetch_rows(tail_ids, neg_ids, ent, conv_weight, conv_bias):
    number = 15
    q = np.arange(FLAT)
    place = np.zeros((8, FLAT), np.int32)
    place[0] = q % 324 // 18
    place[1] = q % 18
    place[2] = q // 324
    wb = jnp.concatenate(
        [conv_weight.reshape(FILTERS, 9).astype(F32), conv_bias[:, None], jnp.zeros((FILTERS, 6), F32)],
        axis=1,
    ).T
    return pl.pallas_call(
        rows_kernel,
        out_shape=(
            jax.ShapeDtypeStruct((TRI, D), BF16),
            jax.ShapeDtypeStruct((2, 2, 8, NEG, D), BF16),
            jax.ShapeDtypeStruct((STEPS, 2, WIDE, CHUNK), BF16),
            jax.ShapeDtypeStruct((STEPS, 1, CHUNK), F32),
            jax.ShapeDtypeStruct((2, TRI), jnp.int32),
            jax.ShapeDtypeStruct((2, NEG), jnp.int32),
        ),
        in_specs=[VMEM_SPEC] * 5,
        out_specs=(
            VMEM_SPEC, VMEM_SPEC, pl.BlockSpec(memory_space=pl.ANY), VMEM_SPEC, VMEM_SPEC, VMEM_SPEC,
        ),
        scratch_shapes=[
            pltpu.VMEM((2, 2, TRI), jnp.int32),
            pltpu.VMEM((2, 2, NEG), jnp.int32),
            pltpu.VMEM((TRI, D), BF16),
            pltpu.VMEM((NEG, D), BF16),
            pltpu.VMEM((TRI, D), BF16),
            pltpu.VMEM((2, 2, 8, NEG, D), BF16),
            pltpu.VMEM((3, 24, CHUNK), F32),
            pltpu.VMEM((STEPS, 2, WIDE, CHUNK), BF16),
            pltpu.SemaphoreType.DMA((STEPS,)),
            pltpu.SemaphoreType.DMA((number,)),
            pltpu.SemaphoreType.DMA((number,)),
        ],
        compiler_params=pltpu.CompilerParams(
            collective_id=0, has_side_effects=True, vmem_limit_bytes=40 << 20
        ),
        name="fetch_rows",
    )(tail_ids, neg_ids, ent, jnp.asarray(place), wb)


def step_of(rows, state, gradient):
    state = state + jnp.sum(gradient * gradient, axis=0, keepdims=True) * (1.0 / D)
    return rows - learn_rate * gradient * lax.rsqrt(state), state


def update_kernel(
    bit, more,
    rel_part, neg_part, tail_grad, head_grad, ent, ent_state, rel, rel_state, head_ids, asked_tail, asked_neg,
    *rest,
):
    if more:
        (ent_out, ent_state_out, rel_out, rel_state_out, tail_out, neg_out), rest = rest[:6], rest[6:]
    else:
        (ent_out, ent_state_out, rel_out, rel_state_out), rest = rest[:4], rest[4:]
    (r0, s1_send, s1_recv, acc1, s2_recv, z_buf, g_buf,
     b1, b2_send, b2_recv, b3_send, b3_recv, b4_send, b4_recv, tail_in), rest = rest[:15], rest[15:]
    if more:
        (pick_tail, pick_neg, tails, negs), rest = rest[:4], rest[4:]
    send, recv = rest
    me = Place()
    copies = Copies(send, recv)
    c, z, y_lo = me.core, me.z, me.y_lo
    first = me.x * (1 - c) + me.y * c
    second = me.y * (1 - c) + me.x * c

    def along_first(i):
        return me.at(x=i * (1 - c) + me.x * c, y=i * c + me.y * (1 - c))

    def along_second(i):
        return me.at(x=me.x * (1 - c) + i * c, y=i * (1 - c) + me.y * c)

    firsts = [(first + d) % 4 for d in range(1, 4)]
    seconds = [(second + d) % 4 for d in range(1, 4)]
    zs = [(z + d) % 8 for d in range(1, 8)]
    mate, partner = me.mate(), me.partner(bit)
    greet(
        [mate]
        + [along_first(i) for i in firsts]
        + [along_second(i) for i in seconds]
        + [me.at(z=i) for i in zs]
    )
    b1_copy = copies.start(neg_part.at[1 - c], b1, mate)
    s0_copy = copies.start(rel_part.at[1 - c], r0, mate)
    tail_copy = copies.start(tail_grad, tail_in, partner)
    b1_copy.wait()
    b2_send[...] = (neg_part[c, 1 - y_lo].astype(F32) + b1[1 - y_lo].astype(F32)).astype(BF16)
    b2_copy = copies.start(b2_send, b2_recv, me.beside())
    s0_copy.wait()
    for i in range(4):
        s1_send[i] = (rel_part[c, i].astype(F32) + r0[i].astype(F32)).astype(BF16)
    s1_copies = [
        copies.start(s1_send.at[i], s1_recv.at[d], along_first(i)) for d, i in enumerate(firsts)
    ]
    b2_copy.wait()
    b3_send[...] = (
        neg_part[c, y_lo].astype(F32) + b1[y_lo].astype(F32) + b2_recv[...].astype(F32)
    ).astype(BF16)
    b3_copies = [
        copies.start(b3_send.at[i], b3_recv.at[d], me.at(z=i)) for d, i in enumerate(zs)
    ]
    wait_all(s1_copies)
    acc1[...] = (
        rel_part[c, first].astype(F32)
        + r0[first].astype(F32)
        + s1_recv[0].astype(F32)
        + s1_recv[1].astype(F32)
        + s1_recv[2].astype(F32)
    )
    s2_copies = [
        copies.start(acc1.at[i], s2_recv.at[d], along_second(i)) for d, i in enumerate(seconds)
    ]
    wait_all(s2_copies)
    z_buf[z] = (acc1[second] + s2_recv[0] + s2_recv[1] + s2_recv[2]).astype(BF16)
    z_copies = [copies.start(z_buf.at[z], z_buf.at[z], me.at(z=i)) for i in zs]
    wait_all(b3_copies)
    share = b3_send[z].astype(F32)
    for d in range(7):
        share = share + b3_recv[d].astype(F32)
    b4_send[...] = share
    b4_copy = copies.start(b4_send, b4_recv, partner)
    wait_all(z_copies)
    total = z_buf[0].astype(F32)
    for i in range(1, 8):
        total = total + z_buf[i].astype(F32)
    g_buf[c, first, second] = total.astype(BF16)
    own = g_buf.at[c, first, second]
    s4_copies = [copies.start(own, own, along_second(i)) for i in seconds]
    b4_copy.wait()
    tail_copy.wait()
    gradient = (
        spread_nt_right(head_grad[...], hot_rows(head_ids[bit : bit + 1, :], ENT))
        + spread_nt_right(tail_in[...], hot_rows(asked_tail[bit : bit + 1, :], ENT))
        + spread_nt_right(b4_recv[...].T, hot_rows(asked_neg[bit : bit + 1, :], ENT))
    )
    new_rows, new_state = step_of(ent[...], ent_state[...], gradient)
    ent_out[...] = new_rows
    ent_state_out[...] = new_state
    if more:
        pick_rows(asked_tail[1:2, :], asked_neg[1:2, :], new_rows.astype(BF16), pick_tail, pick_neg)
        following = me.partner(1 - bit)
        mine = negs.at[c, y_lo, z]
        a1_copy = copies.start(pick_neg, mine, following)
        a0_copy = copies.start(pick_tail, tails, following)
    wait_all(s4_copies)
    own = g_buf.at[c, first]
    s5_copies = [copies.start(own, own, along_first(i)) for i in firsts]
    if more:
        a1_copy.wait()
        a2_copies = [copies.start(mine, mine, me.at(z=i)) for i in zs]
    wait_all(s5_copies)
    own = g_buf.at[c]
    s6_copy = copies.start(own, own, mate)
    if more:
        wait_all(a2_copies)
        half = negs.at[c, y_lo]
        a3_copy = copies.start(half, half, me.beside())
    s6_copy.wait()
    eye = jnp.where(
        lax.broadcasted_iota(jnp.int32, (D, D), 0) == lax.broadcasted_iota(jnp.int32, (D, D), 1), 1.0, 0.0
    ).astype(BF16)
    gradient = nt(eye, g_buf[...].reshape(REL_PAD, D))[:, :REL]
    new_rows, new_state = step_of(rel[...], rel_state[...], gradient)
    rel_out[...] = new_rows
    rel_state_out[...] = new_state
    if more:
        a3_copy.wait()
        half = negs.at[c]
        copies.start(half, half, mate).wait()
        a0_copy.wait()
        tail_out[...] = tails[...]
        neg_out[...] = negs[...]


def update(
    bit, more, rel_part, neg_part, tail_grad, head_grad, ent, ent_state, rel, rel_state,
    head_ids, asked_tail, asked_neg,
):
    out_shape = [
        jax.ShapeDtypeStruct((D, ENT), F32),
        jax.ShapeDtypeStruct((1, ENT), F32),
        jax.ShapeDtypeStruct((D, REL), F32),
        jax.ShapeDtypeStruct((1, REL), F32),
    ]
    scratch = [
        pltpu.VMEM((4, 4, BLK, D), BF16),
        pltpu.VMEM((4, 4, BLK, D), BF16),
        pltpu.VMEM((3, 4, BLK, D), BF16),
        pltpu.VMEM((4, BLK, D), F32),
        pltpu.VMEM((3, BLK, D), F32),
        pltpu.VMEM((8, BLK, D), BF16),
        pltpu.VMEM((2, 4, 4, BLK, D), BF16),
        pltpu.VMEM((2, 8, NEG, D), BF16),
        pltpu.VMEM((8, NEG, D), BF16),
        pltpu.VMEM((8, NEG, D), BF16),
        pltpu.VMEM((8, NEG, D), BF16),
        pltpu.VMEM((7, NEG, D), BF16),
        pltpu.VMEM((NEG, D), F32),
        pltpu.VMEM((NEG, D), F32),
        pltpu.VMEM((D, TRI), F32),
    ]
    operands = [
        rel_part.reshape(2, 4, 4, BLK, D),
        neg_part.reshape(2, 2, 8, NEG, D),
        tail_grad, head_grad, ent, ent_state, rel, rel_state, head_ids, asked_tail, asked_neg,
    ]
    number = 1 + 1 + 1 + 1 + 3 + 7 + 3 + 7 + 1 + 3 + 3 + 1
    if more:
        number += 2 + 7 + 1 + 1
        out_shape += [
            jax.ShapeDtypeStruct((TRI, D), BF16),
            jax.ShapeDtypeStruct((2, 2, 8, NEG, D), BF16),
        ]
        scratch += [
            pltpu.VMEM((TRI, D), BF16),
            pltpu.VMEM((NEG, D), BF16),
            pltpu.VMEM((TRI, D), BF16),
            pltpu.VMEM((2, 2, 8, NEG, D), BF16),
        ]
    scratch += [pltpu.SemaphoreType.DMA((number,)), pltpu.SemaphoreType.DMA((number,))]
    return pl.pallas_call(
        functools.partial(update_kernel, bit, more),
        out_shape=tuple(out_shape),
        in_specs=[VMEM_SPEC] * len(operands),
        out_specs=tuple([VMEM_SPEC] * len(out_shape)),
        scratch_shapes=scratch,
        compiler_params=pltpu.CompilerParams(
            collective_id=1 + bit, has_side_effects=True, vmem_limit_bytes=40 << 20
        ),
        name="update",
    )(*operands)


def shards(
    entity_rows, entity_state, relation_rows, relation_state,
    conv_weight, conv_bias, fc_weight, fc_bias,
    head_ids, rel_ids, tail_ids, neg_ids,
):
    ent, ent_state = entity_rows.T, entity_state.reshape(1, ENT)
    rel, rel_state = relation_rows.T, relation_state.reshape(1, REL)
    w_mat = fc_weight.T
    tails, negset, t_mat, bias, asked_tail, asked_neg = fetch_rows(tail_ids, neg_ids, ent, conv_weight, conv_bias)
    for r in range(2):
        head_grad, rel_part, neg_part, tail_grad = block_pass(
            r, head_ids, rel_ids, ent, rel, t_mat, w_mat, bias, fc_bias.reshape(1, D),
            tails, negset.reshape(1024, D),
        )
        out = update(
            r, r == 0, rel_part, neg_part, tail_grad, head_grad,
            ent, ent_state, rel, rel_state, head_ids, asked_tail, asked_neg,
        )
        ent, ent_state, rel, rel_state = out[:4]
        if r == 0:
            tails, negset = out[4:]
    return ent.T, ent_state.reshape(ENT), rel.T, rel_state.reshape(REL)


def solution(mesh):
    both = ("group", "shard")
    in_specs = (
        P(both, None), P(both), P(), P(), P(), P(), P(), P(),
        P(None, both), P(None, both), P(None, both), P(None, both),
    )
    out_specs = (P(both, None), P(both), P(), P())
    return jax.shard_map(shards, mesh=mesh, in_specs=in_specs, out_specs=out_specs, check_vma=False)
```

```python
import jax
import jax.numpy as jnp
import numpy as np
from jax import lax
from jax.experimental import pallas as pl
from jax.experimental.pallas import tpu as pltpu
from jax.sharding import PartitionSpec as P

D = 200
FILTERS = 32
FLAT = 10368
REL = 1387
REL_PAD = 1536
BLK = 48
TRI = 128
NEG = 32
ENT = 1024
CHUNK = 1152
STEPS = FLAT // CHUNK
WIDE = 240
MESH = pl.DeviceIdType.MESH
F32 = jnp.float32
BF16 = jnp.bfloat16

negative_weight = 0.03125
learn_rate = 0.5

NT = (((1,), (1,)), ((), ()))


def nn(a, b):
    return jnp.dot(a, b, preferred_element_type=F32)


def nt(a, b):
    return lax.dot_general(a, b, NT, preferred_element_type=F32)


def spread_dot(one_hot, values):
    high = values.astype(BF16)
    low = (values - high.astype(F32)).astype(BF16)
    return nn(one_hot, high) + nn(one_hot, low)


def hot_rows(ids_row, extent):
    where = lax.broadcasted_iota(jnp.int32, (extent, ids_row.shape[1]), 0)
    return jnp.where(where == ids_row, 1.0, 0.0).astype(BF16)


class Place:
    def __init__(self):
        group = lax.axis_index("group")
        shard = lax.axis_index("shard")
        self.x = group % 4
        self.y_hi = group // 4
        self.y_lo = shard // 16
        self.z = (shard // 2) % 8
        self.core = shard % 2
        self.y = self.y_hi * 2 + self.y_lo

    def at(self, x=None, y=None, z=None, core=None):
        x = self.x if x is None else x
        y = self.y if y is None else y
        z = self.z if z is None else z
        core = self.core if core is None else core
        return ((y // 2) * 4 + x, (y % 2) * 16 + z * 2 + core)

    def mate(self):
        return self.at(core=1 - self.core)

    def beside(self):
        return self.at(y=self.y_hi * 2 + 1 - self.y_lo)

    def partner(self, bit):
        if bit == 0:
            return self.at(x=self.x + 1 - 2 * (self.x % 2))
        return self.at(x=(self.x + 2) % 4)


class Copies:
    def __init__(self, send, recv):
        self.send, self.recv, self.used = send, recv, 0

    def start(self, src, dst, device):
        copy = pltpu.make_async_remote_copy(
            src_ref=src,
            dst_ref=dst,
            send_sem=self.send.at[self.used],
            recv_sem=self.recv.at[self.used],
            device_id=device,
            device_id_type=MESH,
        )
        self.used += 1
        copy.start()
        return copy


def greet(peers):
    barrier = pltpu.get_barrier_semaphore()
    for peer in peers:
        pl.semaphore_signal(barrier, inc=1, device_id=peer, device_id_type=MESH)
    pl.semaphore_wait(barrier, len(peers))


def wait_all(copies):
    for copy in copies:
        copy.wait()


def spacing():
    d = np.arange(D)
    out = np.zeros((D, WIDE), np.float32)
    out[d, d // 20 * 24 + d % 20] = 1.0
    return jnp.asarray(out, BF16)


def features():
    q = np.arange(FLAT).reshape(STEPS, 1, CHUNK)
    return jnp.asarray(np.concatenate([q % 324 // 18, q % 18, q // 324], axis=1).astype(np.int32))


def spread_nt(one_hot, values):
    high = values.astype(BF16)
    low = (values - high.astype(F32)).astype(BF16)
    return nt(one_hot, high) + nt(one_hot, low)


def spread_nt_right(values, one_hot):
    high = values.astype(BF16)
    low = (values - high.astype(F32)).astype(BF16)
    return nt(high, one_hot) + nt(low, one_hot)


def step_of(rows, state, gradient):
    state = state + jnp.sum(gradient * gradient, axis=0, keepdims=True) * (1.0 / D)
    return rows - learn_rate * gradient * lax.rsqrt(state), state


def loop(first, last, body):
    def one(j, carry):
        body(j)
        return carry

    lax.fori_loop(first, last, one, 0)


ROUND_SCRATCH = dict(
    tails=pltpu.VMEM((TRI, D), BF16),
    negs=pltpu.VMEM((2, 2, 8, NEG, D), BF16),
    pick_tail=pltpu.VMEM((TRI, D), BF16),
    pick_neg=pltpu.VMEM((NEG, D), BF16),
    neg_part=pltpu.VMEM((2, 2, 8, NEG, D), BF16),
    tail_grad=pltpu.VMEM((D, TRI), F32),
    tail_in=pltpu.VMEM((D, TRI), F32),
    b1=pltpu.VMEM((2, 8, NEG, D), BF16),
    b2_send=pltpu.VMEM((8, NEG, D), BF16),
    b2_recv=pltpu.VMEM((8, NEG, D), BF16),
    b3_send=pltpu.VMEM((8, NEG, D), BF16),
    b3_recv=pltpu.VMEM((7, NEG, D), BF16),
    b4_send=pltpu.VMEM((NEG, D), F32),
    b4_recv=pltpu.VMEM((NEG, D), F32),
    s0_send=pltpu.VMEM((4, 4, BLK, D), BF16),
    s0_recv=pltpu.VMEM((4, 4, BLK, D), BF16),
    s1_send=pltpu.VMEM((4, 4, BLK, D), BF16),
    s1_recv=pltpu.VMEM((3, 4, BLK, D), BF16),
    acc1=pltpu.VMEM((4, BLK, D), F32),
    s2_recv=pltpu.VMEM((3, BLK, D), F32),
    z_buf=pltpu.VMEM((8, BLK, D), BF16),
    g_buf=pltpu.VMEM((2, 4, 4, BLK, D), BF16),
)
SHARED_SCRATCH = dict(
    tails_in=pltpu.VMEM((2, 2, TRI), jnp.int32),
    negs_in=pltpu.VMEM((2, 2, NEG), jnp.int32),
    columns=pltpu.VMEM((3, 24, CHUNK), F32),
    t_all=pltpu.VMEM((STEPS, 2, WIDE, CHUNK), BF16),
    w_all=pltpu.VMEM((STEPS, D, CHUNK), BF16),
    bias=pltpu.VMEM((STEPS, 1, CHUNK), F32),
    slope=pltpu.VMEM((STEPS, TRI, CHUNK), F32),
    pic_h=pltpu.VMEM((TRI, WIDE), BF16),
    pic_r=pltpu.VMEM((TRI, WIDE), BF16),
    acc=pltpu.VMEM((TRI, D), F32),
    grad_h=pltpu.VMEM((TRI, WIDE), F32),
    grad_r=pltpu.VMEM((TRI, WIDE), F32),
    pre2_grad=pltpu.VMEM((TRI, D), BF16),
    own_part=pltpu.VMEM((4, 4, BLK, D), F32),
)
COPIES = 4 + 2 * (2 + 7 + 1 + 1) + 2 * (1 + 1 + 1 + 7 + 1 + 1 + 3 + 3 + 7 + 3 + 3 + 1)


class Bag:
    def __init__(self, names, refs):
        self.__dict__.update(zip(names, refs))


def window_kernel(
    head_ids, rel_ids, tail_ids, neg_ids, ent_in, ent_state_in, rel_in, rel_state_in,
    conv_w, conv_b, w_hbm, fc_bias, place_ref, space_ref,
    ent, ent_state, rel, rel_state, *rest,
):
    own = Bag(SHARED_SCRATCH, rest)
    rest = rest[len(SHARED_SCRATCH):]
    rounds = []
    for r in range(2):
        rounds.append(Bag(ROUND_SCRATCH, rest))
        rest = rest[len(ROUND_SCRATCH):]
    w_sem, send, recv = rest
    me = Place()
    copies = Copies(send, recv)
    c, z, y_lo = me.core, me.z, me.y_lo
    first = me.x * (1 - c) + me.y * c
    second = me.y * (1 - c) + me.x * c

    def along_first(i):
        return me.at(x=i * (1 - c) + me.x * c, y=i * c + me.y * (1 - c))

    def along_second(i):
        return me.at(x=me.x * (1 - c) + i * c, y=i * (1 - c) + me.y * c)

    firsts = [(first + d) % 4 for d in range(1, 4)]
    seconds = [(second + d) % 4 for d in range(1, 4)]
    zs = [(z + d) % 8 for d in range(1, 8)]
    mate, beside = me.mate(), me.beside()
    partners = [me.partner(0), me.partner(1)]

    w_copies = []
    for j in range(STEPS):
        copy = pltpu.make_async_copy(
            w_hbm.at[:, pl.ds(j * CHUNK, CHUNK)], own.w_all.at[j], w_sem.at[j]
        )
        copy.start()
        w_copies.append(copy)
    greet(
        [mate]
        + [along_first(i) for i in firsts]
        + [along_second(i) for i in seconds]
        + [me.at(z=i) for i in zs]
    )
    asked = [
        (
            copies.start(tail_ids, own.tails_in.at[r], partners[r]),
            copies.start(neg_ids, own.negs_in.at[r], partners[r]),
        )
        for r in range(2)
    ]

    def build(j):
        down, across, filt = (place_ref[j, k : k + 1, :] for k in range(3))
        hot = lax.broadcasted_iota(jnp.int32, (FILTERS, CHUNK), 0) == filt
        own.bias[j] = jnp.dot(
            conv_b[...], jnp.where(hot, 1.0, 0.0).astype(F32),
            precision=lax.Precision.HIGHEST, preferred_element_type=F32,
        )
        hot = jnp.where(hot, 1.0, 0.0).astype(BF16)
        apart = lax.broadcasted_iota(jnp.int32, (24, CHUNK), 0) - across
        for a in range(3):
            wide = nn(conv_w[a], hot)
            out = jnp.zeros((24, CHUNK), F32)
            for k in range(3):
                out = jnp.where(apart == k, wide[k : k + 1, :], out)
            own.columns[a] = out
        for half in range(2):

            def pair(p):
                rows = []
                for one in range(2):
                    away = (10 * half + 2 * p + one) - down
                    out = jnp.where(away == 2, own.columns[2], 0.0)
                    out = jnp.where(away == 1, own.columns[1], out)
                    rows.append(jnp.where(away == 0, own.columns[0], out))
                low = pl.multiple_of(p * 48, 48)
                own.t_all[j, half, pl.ds(low, 48), :] = jnp.concatenate(rows, axis=0).astype(BF16)

            loop(0, 5, pair)

    def forward(j):
        pre1 = nn(own.pic_h[...], own.t_all[j, 0]) + nn(own.pic_r[...], own.t_all[j, 1]) + own.bias[j]
        sigma = 0.5 * jnp.tanh(0.5 * pre1) + 0.5
        act = pre1 * sigma
        own.slope[j] = sigma + act * (1.0 - sigma)
        own.acc[...] += nt(act.astype(BF16), own.w_all[j])

    def backward(j):
        act_grad = nn(own.pre2_grad[...], own.w_all[j])
        pre1_grad = (act_grad * own.slope[j]).astype(BF16)
        own.grad_h[...] += nt(pre1_grad, own.t_all[j, 0])
        own.grad_r[...] += nt(pre1_grad, own.t_all[j, 1])

    def pick_heads(r, table):
        heads = nn(table, hot_rows(head_ids[r : r + 1, :], ENT))
        own.pic_h[...] = nn(heads.T.astype(BF16), space_ref[...]).astype(BF16)

    def pick_relations(r, table):
        relations = nn(table, hot_rows(rel_ids[r : r + 1, :], REL))
        own.pic_r[...] = nn(relations.T.astype(BF16), space_ref[...]).astype(BF16)

    def rows_go(r, table):
        b = rounds[r]
        b.pick_neg[...] = nn(table, hot_rows(own.negs_in[r, r : r + 1, :], ENT)).T.astype(BF16)
        b.pick_tail[...] = nn(table, hot_rows(own.tails_in[r, r : r + 1, :], ENT)).T.astype(BF16)
        slot = b.negs.at[c, y_lo, z]
        return (
            copies.start(b.pick_neg, slot, partners[r]),
            copies.start(b.pick_tail, b.tails, partners[r]),
        )

    def negs_along_z(r):
        slot = rounds[r].negs.at[c, y_lo, z]
        return [copies.start(slot, slot, me.at(z=i)) for i in zs]

    def negs_beside(r):
        half = rounds[r].negs.at[c, y_lo]
        return copies.start(half, half, beside)

    def negs_to_mate(r):
        half = rounds[r].negs.at[c]
        return copies.start(half, half, mate)

    loop(0, 2, build)
    for pair in asked:
        wait_all(pair)
    table = ent_in[...].astype(BF16)
    neg_go, tail_go = rows_go(0, table)
    pick_heads(0, table)
    pick_relations(0, rel_in[...].astype(BF16))
    loop(2, 4, build)
    neg_go.wait()
    along = negs_along_z(0)
    loop(4, STEPS, build)
    wait_all(along)
    near = negs_beside(0)
    wait_all(w_copies)
    own.acc[...] = jnp.zeros_like(own.acc)
    loop(0, 5, forward)
    near.wait()
    near = negs_to_mate(0)
    loop(5, STEPS, forward)
    near.wait()
    tail_go.wait()

    for r in range(2):
        b = rounds[r]
        more = r == 0
        if r == 1:
            own.acc[...] = jnp.zeros_like(own.acc)
            loop(0, STEPS, forward)
        pre2 = own.acc[...] + fc_bias[...]
        sigma = jax.nn.sigmoid(pre2)
        query = (pre2 * sigma).astype(BF16)
        tails = b.tails[...].astype(F32)
        wide = query.astype(F32)
        pos_grad = -jax.nn.sigmoid(-jnp.sum(wide * tails, axis=1, keepdims=True))
        negset = b.negs[...].reshape(1024, D)
        by_neg = (negative_weight * jax.nn.sigmoid(nt(negset, query))).astype(BF16)
        b.neg_part[...] = nn(by_neg, query).astype(BF16).reshape(2, 2, 8, NEG, D)
        b1_copy = copies.start(b.neg_part.at[1 - c], b.b1, mate)
        b.tail_grad[...] = (pos_grad * wide).T
        tail_copy = copies.start(b.tail_grad, b.tail_in, partners[r])
        by_row = (negative_weight * jax.nn.sigmoid(nt(query, negset))).astype(BF16)
        query_grad = pos_grad * tails + nn(by_row, negset)
        own.pre2_grad[...] = (query_grad * (sigma * (1.0 + pre2 * (1.0 - sigma)))).astype(BF16)
        own.grad_h[...] = jnp.zeros_like(own.grad_h)
        own.grad_r[...] = jnp.zeros_like(own.grad_r)
        loop(0, 3, backward)
        b1_copy.wait()
        b.b2_send[...] = (b.neg_part[c, 1 - y_lo].astype(F32) + b.b1[1 - y_lo].astype(F32)).astype(BF16)
        b2_copy = copies.start(b.b2_send, b.b2_recv, beside)
        loop(3, 6, backward)
        b2_copy.wait()
        b.b3_send[...] = (
            b.neg_part[c, y_lo].astype(F32) + b.b1[y_lo].astype(F32) + b.b2_recv[...].astype(F32)
        ).astype(BF16)
        b3_copies = [
            copies.start(b.b3_send.at[i], b.b3_recv.at[d], me.at(z=i)) for d, i in enumerate(zs)
        ]
        loop(6, STEPS, backward)
        relation_grad = spread_nt_right(own.grad_r[...], space_ref[...])
        rel_row = rel_ids[r : r + 1, :]
        half = REL_PAD // 2

        def part_of(core):
            where = lax.broadcasted_iota(jnp.int32, (half, TRI), 0) + core * half
            hot = jnp.where(where == rel_row, 1.0, 0.0).astype(BF16)
            return spread_dot(hot, relation_grad).reshape(4, 4, BLK, D)

        b.s0_send[...] = part_of(1 - c).astype(BF16)
        s0_copy = copies.start(b.s0_send, b.s0_recv, mate)
        own.own_part[...] = part_of(c)
        wait_all(b3_copies)
        share = b.b3_send[z].astype(F32)
        for d in range(7):
            share = share + b.b3_recv[d].astype(F32)
        b.b4_send[...] = share
        b4_copy = copies.start(b.b4_send, b.b4_recv, partners[r])
        s0_copy.wait()
        for i in range(4):
            b.s1_send[i] = (own.own_part[i] + b.s0_recv[i].astype(F32)).astype(BF16)
        s1_copies = [
            copies.start(b.s1_send.at[i], b.s1_recv.at[d], along_first(i)) for d, i in enumerate(firsts)
        ]
        head_grad = spread_nt(space_ref[...], own.grad_h[...])
        gradient = spread_nt_right(head_grad, hot_rows(head_ids[r : r + 1, :], ENT))
        tail_copy.wait()
        b4_copy.wait()
        gradient = (
            gradient
            + spread_nt_right(b.tail_in[...], hot_rows(own.tails_in[r, r : r + 1, :], ENT))
            + spread_nt_right(b.b4_recv[...].T, hot_rows(own.negs_in[r, r : r + 1, :], ENT))
        )
        if more:
            new_rows, new_state = step_of(ent_in[...], ent_state_in[...], gradient)
        else:
            new_rows, new_state = step_of(ent[...], ent_state[...], gradient)
        ent[...] = new_rows
        ent_state[...] = new_state
        wait_all(s1_copies)
        b.acc1[...] = (
            own.own_part[first]
            + b.s0_recv[first].astype(F32)
            + b.s1_recv[0].astype(F32)
            + b.s1_recv[1].astype(F32)
            + b.s1_recv[2].astype(F32)
        )
        s2_copies = [
            copies.start(b.acc1.at[i], b.s2_recv.at[d], along_second(i)) for d, i in enumerate(seconds)
        ]
        if more:
            table = ent[...].astype(BF16)
            neg_go, tail_go = rows_go(1, table)
        wait_all(s2_copies)
        b.z_buf[z] = (b.acc1[second] + b.s2_recv[0] + b.s2_recv[1] + b.s2_recv[2]).astype(BF16)
        z_copies = [copies.start(b.z_buf.at[z], b.z_buf.at[z], me.at(z=i)) for i in zs]
        if more:
            pick_heads(1, table)
            neg_go.wait()
            along = negs_along_z(1)
        wait_all(z_copies)
        total = b.z_buf[0].astype(F32)
        for i in range(1, 8):
            total = total + b.z_buf[i].astype(F32)
        b.g_buf[c, first, second] = total.astype(BF16)
        slot = b.g_buf.at[c, first, second]
        s4_copies = [copies.start(slot, slot, along_second(i)) for i in seconds]
        if more:
            wait_all(along)
            near = negs_beside(1)
        wait_all(s4_copies)
        slot = b.g_buf.at[c, first]
        s5_copies = [copies.start(slot, slot, along_first(i)) for i in firsts]
        if more:
            near.wait()
            near = negs_to_mate(1)
        wait_all(s5_copies)
        slot = b.g_buf.at[c]
        s6_copy = copies.start(slot, slot, mate)
        eye = jnp.where(
            lax.broadcasted_iota(jnp.int32, (D, D), 0) == lax.broadcasted_iota(jnp.int32, (D, D), 1), 1.0, 0.0
        ).astype(BF16)
        s6_copy.wait()
        gradient = nt(eye, b.g_buf[...].reshape(REL_PAD, D))[:, :REL]
        if more:
            new_rows, new_state = step_of(rel_in[...], rel_state_in[...], gradient)
        else:
            new_rows, new_state = step_of(rel[...], rel_state[...], gradient)
        rel[...] = new_rows
        rel_state[...] = new_state
        if more:
            pick_relations(1, new_rows.astype(BF16))
            near.wait()
            tail_go.wait()


def shards(
    entity_rows, entity_state, relation_rows, relation_state,
    conv_weight, conv_bias, fc_weight, fc_bias,
    head_ids, rel_ids, tail_ids, neg_ids,
):
    vmem = pl.BlockSpec(memory_space=pltpu.VMEM)
    operands = [
        head_ids, rel_ids, tail_ids, neg_ids,
        entity_rows.T, entity_state.reshape(1, ENT), relation_rows.T, relation_state.reshape(1, REL),
        jnp.transpose(conv_weight, (1, 2, 0)), conv_bias.reshape(1, FILTERS),
        fc_weight.T, fc_bias.reshape(1, D), features(), spacing(),
    ]
    specs = [vmem] * len(operands)
    specs[10] = pl.BlockSpec(memory_space=pl.ANY)
    ent, ent_state, rel, rel_state = pl.pallas_call(
        window_kernel,
        out_shape=(
            jax.ShapeDtypeStruct((D, ENT), F32),
            jax.ShapeDtypeStruct((1, ENT), F32),
            jax.ShapeDtypeStruct((D, REL), F32),
            jax.ShapeDtypeStruct((1, REL), F32),
        ),
        in_specs=specs,
        out_specs=(vmem,) * 4,
        scratch_shapes=[
            *SHARED_SCRATCH.values(),
            *ROUND_SCRATCH.values(),
            *ROUND_SCRATCH.values(),
            pltpu.SemaphoreType.DMA((STEPS,)),
            pltpu.SemaphoreType.DMA((COPIES,)),
            pltpu.SemaphoreType.DMA((COPIES,)),
        ],
        compiler_params=pltpu.CompilerParams(
            collective_id=0, has_side_effects=True, vmem_limit_bytes=60 << 20
        ),
        name="window",
    )(*operands)
    return ent.T, ent_state.reshape(ENT), rel.T, rel_state.reshape(REL)


def solution(mesh):
    both = ("group", "shard")
    in_specs = (
        P(both, None), P(both), P(), P(), P(), P(), P(), P(),
        P(None, both), P(None, both), P(None, both), P(None, both),
    )
    out_specs = (P(both, None), P(both), P(), P())
    return jax.shard_map(shards, mesh=mesh, in_specs=in_specs, out_specs=out_specs, check_vma=False)
```

```python
import jax
import jax.numpy as jnp
import numpy as np
from jax import lax
from jax.experimental import pallas as pl
from jax.experimental.pallas import tpu as pltpu
from jax.sharding import PartitionSpec as P

D = 200
FILTERS = 32
FLAT = 10368
REL = 1387
REL_PAD = 1536
BLK = 48
TRI = 128
NEG = 32
ENT = 1024
CHUNK = 1152
STEPS = FLAT // CHUNK
WIDE = 240
LANES = 256
MESH = pl.DeviceIdType.MESH
F32 = jnp.float32
BF16 = jnp.bfloat16

negative_weight = 0.03125
learn_rate = 0.5

NT = (((1,), (1,)), ((), ()))


def nn(a, b):
    return jnp.dot(a, b, preferred_element_type=F32)


def nt(a, b):
    return lax.dot_general(a, b, NT, preferred_element_type=F32)


def spread_dot(one_hot, values):
    high = values.astype(BF16)
    low = (values - high.astype(F32)).astype(BF16)
    return nn(one_hot, high) + nn(one_hot, low)


def hot_rows(ids_row, extent):
    where = lax.broadcasted_iota(jnp.int32, (extent, ids_row.shape[1]), 0)
    return jnp.where(where == ids_row, 1.0, 0.0).astype(BF16)


class Place:
    def __init__(self):
        group = lax.axis_index("group")
        shard = lax.axis_index("shard")
        self.x = group % 4
        self.y_hi = group // 4
        self.y_lo = shard // 16
        self.z = (shard // 2) % 8
        self.core = shard % 2
        self.y = self.y_hi * 2 + self.y_lo

    def at(self, x=None, y=None, z=None, core=None):
        x = self.x if x is None else x
        y = self.y if y is None else y
        z = self.z if z is None else z
        core = self.core if core is None else core
        return ((y // 2) * 4 + x, (y % 2) * 16 + z * 2 + core)

    def mate(self):
        return self.at(core=1 - self.core)

    def beside(self):
        return self.at(y=self.y_hi * 2 + 1 - self.y_lo)

    def partner(self, bit):
        if bit == 0:
            return self.at(x=self.x + 1 - 2 * (self.x % 2))
        return self.at(x=(self.x + 2) % 4)


class Copies:
    def __init__(self, send, recv):
        self.send, self.recv, self.used = send, recv, 0

    def start(self, src, dst, device):
        copy = pltpu.make_async_remote_copy(
            src_ref=src,
            dst_ref=dst,
            send_sem=self.send.at[self.used],
            recv_sem=self.recv.at[self.used],
            device_id=device,
            device_id_type=MESH,
        )
        self.used += 1
        copy.start()
        return copy


def greet(peers):
    barrier = pltpu.get_barrier_semaphore()
    for peer in peers:
        pl.semaphore_signal(barrier, inc=1, device_id=peer, device_id_type=MESH)
    pl.semaphore_wait(barrier, len(peers))


def wait_all(copies):
    for copy in copies:
        copy.wait()


def spacing():
    d = np.arange(D)
    out = np.zeros((LANES, WIDE), np.float32)
    out[d, d // 20 * 24 + d % 20] = 1.0
    return jnp.asarray(out, BF16)


def features():
    q = np.arange(FLAT).reshape(STEPS, 1, CHUNK)
    return jnp.asarray(np.concatenate([q % 324 // 18, q % 18, q // 324], axis=1).astype(np.int32))


def spread_nt(one_hot, values):
    high = values.astype(BF16)
    low = (values - high.astype(F32)).astype(BF16)
    return nt(one_hot, high) + nt(one_hot, low)


def spread_nt_right(values, one_hot):
    high = values.astype(BF16)
    low = (values - high.astype(F32)).astype(BF16)
    return nt(high, one_hot) + nt(low, one_hot)


def step_of(rows, state, gradient):
    state = state + jnp.sum(gradient * gradient, axis=0, keepdims=True) * (1.0 / D)
    return rows - learn_rate * gradient * lax.rsqrt(state), state


def widen():
    row = lax.broadcasted_iota(jnp.int32, (D, LANES), 0)
    return jnp.where(row == lax.broadcasted_iota(jnp.int32, (D, LANES), 1), 1.0, 0.0).astype(BF16)


def loop(first, last, body):
    def one(j, carry):
        body(j)
        return carry

    lax.fori_loop(first, last, one, 0)


ROUND_SCRATCH = dict(
    tails=pltpu.VMEM((TRI, LANES), BF16),
    negs=pltpu.VMEM((2, 2, 8, NEG, LANES), BF16),
    pick_tail=pltpu.VMEM((TRI, LANES), BF16),
    pick_neg=pltpu.VMEM((NEG, LANES), BF16),
    neg_part=pltpu.VMEM((2, 2, 8, NEG, LANES), BF16),
    tail_grad=pltpu.VMEM((D, TRI), F32),
    tail_in=pltpu.VMEM((D, TRI), F32),
    b1=pltpu.VMEM((2, 8, NEG, LANES), BF16),
    b2_send=pltpu.VMEM((8, NEG, LANES), BF16),
    b2_recv=pltpu.VMEM((8, NEG, LANES), BF16),
    b3_send=pltpu.VMEM((8, NEG, LANES), BF16),
    b3_recv=pltpu.VMEM((7, NEG, LANES), BF16),
    b4_send=pltpu.VMEM((NEG, LANES), F32),
    b4_recv=pltpu.VMEM((NEG, LANES), F32),
    s0_send=pltpu.VMEM((4, 4, BLK, LANES), BF16),
    s0_recv=pltpu.VMEM((4, 4, BLK, LANES), BF16),
    s1_send=pltpu.VMEM((4, 4, BLK, LANES), BF16),
    s1_recv=pltpu.VMEM((15, BLK, LANES), BF16),
    z_buf=pltpu.VMEM((8, BLK, LANES), BF16),
    g_buf=pltpu.VMEM((2, 4, 4, BLK, LANES), BF16),
)
SHARED_SCRATCH = dict(
    tails_in=pltpu.VMEM((2, 2, TRI), jnp.int32),
    negs_in=pltpu.VMEM((2, 2, NEG), jnp.int32),
    columns=pltpu.VMEM((3, 24, CHUNK), F32),
    t_all=pltpu.VMEM((STEPS, 2, WIDE, CHUNK), BF16),
    w_all=pltpu.VMEM((STEPS, D, CHUNK), BF16),
    p1=pltpu.VMEM((STEPS, TRI, CHUNK), BF16),
    bias=pltpu.VMEM((STEPS, 1, CHUNK), F32),
    slope=pltpu.VMEM((STEPS, TRI, CHUNK), F32),
    pic_h=pltpu.VMEM((TRI, WIDE), BF16),
    pic_r=pltpu.VMEM((TRI, WIDE), BF16),
    acc=pltpu.VMEM((TRI, D), F32),
    grad_h=pltpu.VMEM((TRI, WIDE), F32),
    grad_r=pltpu.VMEM((TRI, WIDE), F32),
    pre2_grad=pltpu.VMEM((TRI, D), BF16),
    own_part=pltpu.VMEM((4, 4, BLK, LANES), F32),
)
COPIES = 4 + 2 * (2 + 7 + 1 + 1) + 2 * (1 + 1 + 1 + 7 + 1 + 1 + 15 + 7 + 15 + 1)


class Bag:
    def __init__(self, names, refs):
        self.__dict__.update(zip(names, refs))


def window_kernel(
    head_ids, rel_ids, tail_ids, neg_ids, ent_in, ent_state_in, rel_in, rel_state_in,
    conv_w, conv_b, w_hbm, fc_bias, place_ref, space_ref,
    ent, ent_state, rel, rel_state, *rest,
):
    own = Bag(SHARED_SCRATCH, rest)
    rest = rest[len(SHARED_SCRATCH):]
    rounds = []
    for r in range(2):
        rounds.append(Bag(ROUND_SCRATCH, rest))
        rest = rest[len(ROUND_SCRATCH):]
    w_sem, send, recv = rest
    me = Place()
    copies = Copies(send, recv)
    c, z, y_lo = me.core, me.z, me.y_lo
    steps = sorted(
        ((dx, dy) for dx in range(4) for dy in range(4) if dx or dy),
        key=lambda d: -min(d[0], 4 - d[0]) - min(d[1], 4 - d[1]),
    )
    plane = [((me.x + dx) % 4, (me.y + dy) % 4) for dx, dy in steps]
    zs = [(z + d) % 8 for d in range(1, 8)]
    mate, beside = me.mate(), me.beside()
    partners = [me.partner(0), me.partner(1)]

    w_copies = []
    for j in range(STEPS):
        copy = pltpu.make_async_copy(
            w_hbm.at[:, pl.ds(j * CHUNK, CHUNK)], own.w_all.at[j], w_sem.at[j]
        )
        copy.start()
        w_copies.append(copy)
    greet(
        [mate]
        + [me.at(x=i, y=k) for i, k in plane]
        + [me.at(z=i) for i in zs]
    )
    asked = [
        (
            copies.start(tail_ids, own.tails_in.at[r], partners[r]),
            copies.start(neg_ids, own.negs_in.at[r], partners[r]),
        )
        for r in range(2)
    ]

    def build(j):
        down, across, filt = (place_ref[j, k : k + 1, :] for k in range(3))
        hot = lax.broadcasted_iota(jnp.int32, (FILTERS, CHUNK), 0) == filt
        own.bias[j] = jnp.dot(
            conv_b[...], jnp.where(hot, 1.0, 0.0).astype(F32),
            precision=lax.Precision.HIGHEST, preferred_element_type=F32,
        )
        hot = jnp.where(hot, 1.0, 0.0).astype(BF16)
        apart = lax.broadcasted_iota(jnp.int32, (24, CHUNK), 0) - across
        for a in range(3):
            wide = nn(conv_w[a], hot)
            out = jnp.zeros((24, CHUNK), F32)
            for k in range(3):
                out = jnp.where(apart == k, wide[k : k + 1, :], out)
            own.columns[a] = out
        for half in range(2):

            def pair(p):
                rows = []
                for one in range(2):
                    away = (10 * half + 2 * p + one) - down
                    out = jnp.where(away == 2, own.columns[2], 0.0)
                    out = jnp.where(away == 1, own.columns[1], out)
                    rows.append(jnp.where(away == 0, own.columns[0], out))
                low = pl.multiple_of(p * 48, 48)
                own.t_all[j, half, pl.ds(low, 48), :] = jnp.concatenate(rows, axis=0).astype(BF16)

            loop(0, 5, pair)

    def forward_heads(j):
        own.slope[j] = nn(own.pic_h[...], own.t_all[j, 0]) + own.bias[j]

    def forward(j, heads=None):
        pre1 = nn(own.pic_r[...], own.t_all[j, 1])
        if heads is None:
            pre1 = pre1 + nn(own.pic_h[...], own.t_all[j, 0]) + own.bias[j]
        else:
            pre1 = pre1 + heads[j]
        sigma = 0.5 * jnp.tanh(0.5 * pre1) + 0.5
        act = pre1 * sigma
        own.slope[j] = sigma + act * (1.0 - sigma)
        own.acc[...] += nt(act.astype(BF16), own.w_all[j])

    def backward(j):
        act_grad = nn(own.pre2_grad[...], own.w_all[j])
        pre1_grad = (act_grad * own.slope[j]).astype(BF16)
        own.p1[j] = pre1_grad
        own.grad_r[...] += nt(pre1_grad, own.t_all[j, 1])

    def backward_heads(j):
        own.grad_h[...] += nt(own.p1[j], own.t_all[j, 0])

    def pick_heads(r, table):
        heads = nn(table, hot_rows(head_ids[r : r + 1, :], ENT))
        own.pic_h[...] = nn(heads.T.astype(BF16), space_ref[:D, :]).astype(BF16)

    def pick_relations(r, table):
        relations = nn(table, hot_rows(rel_ids[r : r + 1, :], REL))
        own.pic_r[...] = nn(relations.T.astype(BF16), space_ref[:D, :]).astype(BF16)

    def rows_go(r, table):
        b = rounds[r]
        rows = nn(table, hot_rows(own.negs_in[r, r : r + 1, :], ENT)).T.astype(BF16)
        b.pick_neg[...] = nn(rows, widen()).astype(BF16)
        rows = nn(table, hot_rows(own.tails_in[r, r : r + 1, :], ENT)).T.astype(BF16)
        b.pick_tail[...] = nn(rows, widen()).astype(BF16)
        slot = b.negs.at[c, y_lo, z]
        return (
            copies.start(b.pick_neg, slot, partners[r]),
            copies.start(b.pick_tail, b.tails, partners[r]),
        )

    def negs_along_z(r):
        slot = rounds[r].negs.at[c, y_lo, z]
        return [copies.start(slot, slot, me.at(z=i)) for i in zs]

    def negs_beside(r):
        half = rounds[r].negs.at[c, y_lo]
        return copies.start(half, half, beside)

    def negs_to_mate(r):
        half = rounds[r].negs.at[c]
        return copies.start(half, half, mate)

    loop(0, 2, build)
    for pair in asked:
        wait_all(pair)
    table = ent_in[...].astype(BF16)
    neg_go, tail_go = rows_go(0, table)
    pick_heads(0, table)
    pick_relations(0, rel_in[...].astype(BF16))
    loop(2, 4, build)
    neg_go.wait()
    along = negs_along_z(0)
    loop(4, STEPS, build)
    wait_all(along)
    near = negs_beside(0)
    wait_all(w_copies)
    own.acc[...] = jnp.zeros_like(own.acc)
    loop(0, 5, forward)
    near.wait()
    near = negs_to_mate(0)
    loop(5, STEPS, forward)
    near.wait()
    tail_go.wait()

    for r in range(2):
        b = rounds[r]
        more = r == 0
        if r == 1:
            own.acc[...] = jnp.zeros_like(own.acc)
            loop(0, 3, lambda j: forward(j, own.slope))
            near.wait()
            near = negs_to_mate(1)
            loop(3, STEPS, lambda j: forward(j, own.slope))
            near.wait()
            tail_go.wait()
        pre2 = own.acc[...] + fc_bias[...]
        sigma = jax.nn.sigmoid(pre2)
        query = nn((pre2 * sigma).astype(BF16), widen()).astype(BF16)
        tails = b.tails[...].astype(F32)
        wide = query.astype(F32)
        pos_grad = -jax.nn.sigmoid(-jnp.sum(wide * tails, axis=1, keepdims=True))
        negset = b.negs[...].reshape(1024, LANES)
        by_neg = (negative_weight * jax.nn.sigmoid(nt(negset, query))).astype(BF16)
        b.neg_part[...] = nn(by_neg, query).astype(BF16).reshape(2, 2, 8, NEG, LANES)
        b1_copy = copies.start(b.neg_part.at[1 - c], b.b1, mate)
        b.tail_grad[...] = (pos_grad * wide).T[:D]
        tail_copy = copies.start(b.tail_grad, b.tail_in, partners[r])
        by_row = (negative_weight * jax.nn.sigmoid(nt(query, negset))).astype(BF16)
        query_grad = (pos_grad * tails + nn(by_row, negset))[:, :D]
        own.pre2_grad[...] = (query_grad * (sigma * (1.0 + pre2 * (1.0 - sigma)))).astype(BF16)
        own.grad_h[...] = jnp.zeros_like(own.grad_h)
        own.grad_r[...] = jnp.zeros_like(own.grad_r)
        loop(0, 3, backward)
        b1_copy.wait()
        b.b2_send[...] = (b.neg_part[c, 1 - y_lo].astype(F32) + b.b1[1 - y_lo].astype(F32)).astype(BF16)
        b2_copy = copies.start(b.b2_send, b.b2_recv, beside)
        loop(3, 6, backward)
        b2_copy.wait()
        b.b3_send[...] = (
            b.neg_part[c, y_lo].astype(F32) + b.b1[y_lo].astype(F32) + b.b2_recv[...].astype(F32)
        ).astype(BF16)
        b3_copies = [
            copies.start(b.b3_send.at[i], b.b3_recv.at[d], me.at(z=i)) for d, i in enumerate(zs)
        ]
        loop(6, STEPS, backward)
        relation_grad = spread_nt_right(own.grad_r[...], space_ref[...])
        rel_row = rel_ids[r : r + 1, :]
        half = REL_PAD // 2

        def part_of(core):
            where = lax.broadcasted_iota(jnp.int32, (half, TRI), 0) + core * half
            hot = jnp.where(where == rel_row, 1.0, 0.0).astype(BF16)
            return spread_dot(hot, relation_grad).reshape(4, 4, BLK, LANES)

        b.s0_send[...] = part_of(1 - c).astype(BF16)
        s0_copy = copies.start(b.s0_send, b.s0_recv, mate)
        own.own_part[...] = part_of(c)
        wait_all(b3_copies)
        share = b.b3_send[z].astype(F32)
        for d in range(7):
            share = share + b.b3_recv[d].astype(F32)
        b.b4_send[...] = share
        b4_copy = copies.start(b.b4_send, b.b4_recv, partners[r])
        s0_copy.wait()
        b.s1_send[...] = (own.own_part[...] + b.s0_recv[...].astype(F32)).astype(BF16)
        s1_copies = [
            copies.start(b.s1_send.at[i, k], b.s1_recv.at[d], me.at(x=i, y=k))
            for d, (i, k) in enumerate(plane)
        ]
        loop(0, STEPS, backward_heads)
        head_grad = spread_nt(space_ref[:D, :], own.grad_h[...])
        gradient = spread_nt_right(head_grad, hot_rows(head_ids[r : r + 1, :], ENT))
        tail_copy.wait()
        b4_copy.wait()
        gradient = (
            gradient
            + spread_nt_right(b.tail_in[...], hot_rows(own.tails_in[r, r : r + 1, :], ENT))
            + spread_nt_right(b.b4_recv[...].T[:D], hot_rows(own.negs_in[r, r : r + 1, :], ENT))
        )
        if more:
            new_rows, new_state = step_of(ent_in[...], ent_state_in[...], gradient)
        else:
            new_rows, new_state = step_of(ent[...], ent_state[...], gradient)
        ent[...] = new_rows
        ent_state[...] = new_state
        wait_all(s1_copies)
        mine = own.own_part[me.x, me.y] + b.s0_recv[me.x, me.y].astype(F32)
        for d in range(15):
            mine = mine + b.s1_recv[d].astype(F32)
        b.z_buf[z] = mine.astype(BF16)
        z_copies = [copies.start(b.z_buf.at[z], b.z_buf.at[z], me.at(z=i)) for i in zs]
        if more:
            table = ent[...].astype(BF16)
            neg_go, tail_go = rows_go(1, table)
            pick_heads(1, table)
            neg_go.wait()
            along = negs_along_z(1)
            loop(0, STEPS, forward_heads)
        wait_all(z_copies)
        total = b.z_buf[0].astype(F32)
        for i in range(1, 8):
            total = total + b.z_buf[i].astype(F32)
        b.g_buf[c, me.x, me.y] = total.astype(BF16)
        slot = b.g_buf.at[c, me.x, me.y]
        s4_copies = [copies.start(slot, slot, me.at(x=i, y=k)) for i, k in plane]
        if more:
            wait_all(along)
            near = negs_beside(1)
        wait_all(s4_copies)
        slot = b.g_buf.at[c]
        s6_copy = copies.start(slot, slot, mate)
        s6_copy.wait()
        gradient = nt(widen(), b.g_buf[...].reshape(REL_PAD, LANES))[:, :REL]
        if more:
            new_rows, new_state = step_of(rel_in[...], rel_state_in[...], gradient)
        else:
            new_rows, new_state = step_of(rel[...], rel_state[...], gradient)
        rel[...] = new_rows
        rel_state[...] = new_state
        if more:
            pick_relations(1, new_rows.astype(BF16))


def shards(
    entity_rows, entity_state, relation_rows, relation_state,
    conv_weight, conv_bias, fc_weight, fc_bias,
    head_ids, rel_ids, tail_ids, neg_ids,
):
    vmem = pl.BlockSpec(memory_space=pltpu.VMEM)
    operands = [
        head_ids, rel_ids, tail_ids, neg_ids,
        entity_rows.T, entity_state.reshape(1, ENT), relation_rows.T, relation_state.reshape(1, REL),
        jnp.transpose(conv_weight, (1, 2, 0)), conv_bias.reshape(1, FILTERS),
        fc_weight.T, fc_bias.reshape(1, D), features(), spacing(),
    ]
    specs = [vmem] * len(operands)
    specs[10] = pl.BlockSpec(memory_space=pl.ANY)
    ent, ent_state, rel, rel_state = pl.pallas_call(
        window_kernel,
        out_shape=(
            jax.ShapeDtypeStruct((D, ENT), F32),
            jax.ShapeDtypeStruct((1, ENT), F32),
            jax.ShapeDtypeStruct((D, REL), F32),
            jax.ShapeDtypeStruct((1, REL), F32),
        ),
        in_specs=specs,
        out_specs=(vmem,) * 4,
        scratch_shapes=[
            *SHARED_SCRATCH.values(),
            *ROUND_SCRATCH.values(),
            *ROUND_SCRATCH.values(),
            pltpu.SemaphoreType.DMA((STEPS,)),
            pltpu.SemaphoreType.DMA((COPIES,)),
            pltpu.SemaphoreType.DMA((COPIES,)),
        ],
        compiler_params=pltpu.CompilerParams(
            collective_id=0, has_side_effects=True, vmem_limit_bytes=60 << 20
        ),
        name="window",
    )(*operands)
    return ent.T, ent_state.reshape(ENT), rel.T, rel_state.reshape(REL)


def solution(mesh):
    both = ("group", "shard")
    in_specs = (
        P(both, None), P(both), P(), P(), P(), P(), P(), P(),
        P(None, both), P(None, both), P(None, both), P(None, both),
    )
    out_specs = (P(both, None), P(both), P(), P())
    return jax.shard_map(shards, mesh=mesh, in_specs=in_specs, out_specs=out_specs, check_vma=False)
```

```python
import jax
import jax.numpy as jnp
import numpy as np
from jax import lax
from jax.experimental import pallas as pl
from jax.experimental.pallas import tpu as pltpu
from jax.sharding import PartitionSpec as P

D = 200
FILTERS = 32
FLAT = 10368
REL = 1387
REL_PAD = 1536
BLK = 48
TRI = 128
NEG = 32
ENT = 1024
CHUNK = 1152
STEPS = FLAT // CHUNK
WIDE = 240
LANES = 256
MESH = pl.DeviceIdType.MESH
F32 = jnp.float32
BF16 = jnp.bfloat16

negative_weight = 0.03125
learn_rate = 0.5

NT = (((1,), (1,)), ((), ()))


def nn(a, b):
    return jnp.dot(a, b, preferred_element_type=F32)


def nt(a, b):
    return lax.dot_general(a, b, NT, preferred_element_type=F32)


def spread_dot(one_hot, values):
    high = values.astype(BF16)
    low = (values - high.astype(F32)).astype(BF16)
    return nn(one_hot, high) + nn(one_hot, low)


def hot_rows(ids_row, extent):
    where = lax.broadcasted_iota(jnp.int32, (extent, ids_row.shape[1]), 0)
    return jnp.where(where == ids_row, 1.0, 0.0).astype(BF16)


class Place:
    def __init__(self):
        group = lax.axis_index("group")
        shard = lax.axis_index("shard")
        self.x = group % 4
        self.y_hi = group // 4
        self.y_lo = shard // 16
        self.z = (shard // 2) % 8
        self.core = shard % 2
        self.y = self.y_hi * 2 + self.y_lo

    def at(self, x=None, y=None, z=None, core=None):
        x = self.x if x is None else x
        y = self.y if y is None else y
        z = self.z if z is None else z
        core = self.core if core is None else core
        return ((y // 2) * 4 + x, (y % 2) * 16 + z * 2 + core)

    def mate(self):
        return self.at(core=1 - self.core)

    def beside(self):
        return self.at(y=self.y_hi * 2 + 1 - self.y_lo)

    def partner(self, bit):
        if bit == 0:
            return self.at(x=self.x + 1 - 2 * (self.x % 2))
        return self.at(x=(self.x + 2) % 4)


class Copies:
    def __init__(self, send, recv):
        self.send, self.recv, self.used = send, recv, 0

    def start(self, src, dst, device):
        copy = pltpu.make_async_remote_copy(
            src_ref=src,
            dst_ref=dst,
            send_sem=self.send.at[self.used],
            recv_sem=self.recv.at[self.used],
            device_id=device,
            device_id_type=MESH,
        )
        self.used += 1
        copy.start()
        return copy


def greet(peers):
    barrier = pltpu.get_barrier_semaphore()
    for peer in peers:
        pl.semaphore_signal(barrier, inc=1, device_id=peer, device_id_type=MESH)
    pl.semaphore_wait(barrier, len(peers))


def wait_all(copies):
    for copy in copies:
        copy.wait()


def spacing():
    d = np.arange(D)
    out = np.zeros((LANES, WIDE), np.float32)
    out[d, d // 20 * 24 + d % 20] = 1.0
    return jnp.asarray(out, BF16)


def features():
    q = np.arange(FLAT).reshape(STEPS, 1, CHUNK)
    return jnp.asarray(np.concatenate([q % 324 // 18, q % 18, q // 324], axis=1).astype(np.int32))


def spread_nt(one_hot, values):
    high = values.astype(BF16)
    low = (values - high.astype(F32)).astype(BF16)
    return nt(one_hot, high) + nt(one_hot, low)


def spread_nt_right(values, one_hot):
    high = values.astype(BF16)
    low = (values - high.astype(F32)).astype(BF16)
    return nt(high, one_hot) + nt(low, one_hot)


def step_of(rows, state, gradient):
    state = state + jnp.sum(gradient * gradient, axis=0, keepdims=True) * (1.0 / D)
    return rows - learn_rate * gradient * lax.rsqrt(state), state


def widen():
    row = lax.broadcasted_iota(jnp.int32, (D, LANES), 0)
    return jnp.where(row == lax.broadcasted_iota(jnp.int32, (D, LANES), 1), 1.0, 0.0).astype(BF16)


def loop(first, last, body):
    def one(j, carry):
        body(j)
        return carry

    lax.fori_loop(first, last, one, 0)


ROUND_SCRATCH = dict(
    tails=pltpu.VMEM((TRI, LANES), BF16),
    negs=pltpu.VMEM((2, 2, 8, NEG, LANES), BF16),
    pick_tail=pltpu.VMEM((TRI, LANES), BF16),
    pick_neg=pltpu.VMEM((NEG, LANES), BF16),
    neg_part=pltpu.VMEM((2, 2, 8, NEG, LANES), BF16),
    tail_grad=pltpu.VMEM((D, TRI), F32),
    tail_in=pltpu.VMEM((D, TRI), F32),
    b1=pltpu.VMEM((2, 8, NEG, LANES), BF16),
    b2_send=pltpu.VMEM((8, NEG, LANES), BF16),
    b2_recv=pltpu.VMEM((8, NEG, LANES), BF16),
    b3_send=pltpu.VMEM((8, NEG, LANES), BF16),
    b3_recv=pltpu.VMEM((7, NEG, LANES), BF16),
    b4_send=pltpu.VMEM((NEG, LANES), F32),
    b4_recv=pltpu.VMEM((NEG, LANES), F32),
    s0_send=pltpu.VMEM((4, 4, BLK, LANES), BF16),
    s0_recv=pltpu.VMEM((4, 4, BLK, LANES), BF16),
    s1_send=pltpu.VMEM((2, 4, 4, BLK, 128), BF16),
    s1_recv=pltpu.VMEM((2, 15, BLK, 128), BF16),
    z_buf=pltpu.VMEM((2, 8, BLK, 128), BF16),
    g_buf=pltpu.VMEM((2, 2, 4, 4, BLK, 128), BF16),
)
SHARED_SCRATCH = dict(
    tails_in=pltpu.VMEM((2, 2, TRI), jnp.int32),
    negs_in=pltpu.VMEM((2, 2, NEG), jnp.int32),
    columns=pltpu.VMEM((3, 24, CHUNK), F32),
    t_all=pltpu.VMEM((STEPS, 2, WIDE, CHUNK), BF16),
    w_all=pltpu.VMEM((STEPS, D, CHUNK), BF16),
    p1=pltpu.VMEM((STEPS, TRI, CHUNK), BF16),
    bias=pltpu.VMEM((STEPS, 1, CHUNK), F32),
    slope=pltpu.VMEM((STEPS, TRI, CHUNK), F32),
    pic_h=pltpu.VMEM((TRI, WIDE), BF16),
    pic_r=pltpu.VMEM((TRI, WIDE), BF16),
    acc=pltpu.VMEM((TRI, D), F32),
    grad_h=pltpu.VMEM((TRI, WIDE), F32),
    grad_r=pltpu.VMEM((TRI, WIDE), F32),
    pre2_grad=pltpu.VMEM((TRI, D), BF16),
    own_part=pltpu.VMEM((4, 4, BLK, LANES), F32),
    ent_grad=pltpu.VMEM((D, ENT), F32),
)
COPIES = 4 + 2 * (1 + 8 + 1 + 1) + 2 * (1 + 1 + 1 + 7 + 1 + 1 + 2 * (15 + 7 + 15 + 1))


class Bag:
    def __init__(self, names, refs):
        self.__dict__.update(zip(names, refs))


def window_kernel(
    head_ids, rel_ids, tail_ids, neg_ids, ent_in, ent_state_in, rel_in, rel_state_in,
    conv_w, conv_b, w_hbm, fc_bias, place_ref, space_ref,
    ent, ent_state, rel, rel_state, *rest,
):
    own = Bag(SHARED_SCRATCH, rest)
    rest = rest[len(SHARED_SCRATCH):]
    rounds = []
    for r in range(2):
        rounds.append(Bag(ROUND_SCRATCH, rest))
        rest = rest[len(ROUND_SCRATCH):]
    w_sem, send, recv = rest
    me = Place()
    copies = Copies(send, recv)
    c, z, y_lo = me.core, me.z, me.y_lo
    steps = sorted(
        ((dx, dy) for dx in range(4) for dy in range(4) if dx or dy),
        key=lambda d: -min(d[0], 4 - d[0]) - min(d[1], 4 - d[1]),
    )
    plane = [((me.x + dx) % 4, (me.y + dy) % 4) for dx, dy in steps]
    zs = [(z + d) % 8 for d in range(1, 8)]
    mate, beside = me.mate(), me.beside()
    partners = [me.partner(0), me.partner(1)]
    across = [
        lambda i: me.at(x=me.x + 1 - 2 * (me.x % 2), z=i),
        lambda i: me.at(x=(me.x + 2) % 4, z=i),
    ]

    w_copies = []
    for j in range(STEPS):
        copy = pltpu.make_async_copy(
            w_hbm.at[:, pl.ds(j * CHUNK, CHUNK)], own.w_all.at[j], w_sem.at[j]
        )
        copy.start()
        w_copies.append(copy)
    greet(
        [mate]
        + [me.at(x=i, y=k) for i, k in plane]
        + [me.at(z=i) for i in zs]
        + [at(i) for at in across for i in zs]
    )
    asked = [
        (
            copies.start(tail_ids, own.tails_in.at[r], partners[r]),
            copies.start(neg_ids, own.negs_in.at[r], partners[r]),
        )
        for r in range(2)
    ]

    def build(j):
        down, across, filt = (place_ref[j, k : k + 1, :] for k in range(3))
        hot = lax.broadcasted_iota(jnp.int32, (FILTERS, CHUNK), 0) == filt
        own.bias[j] = jnp.dot(
            conv_b[...], jnp.where(hot, 1.0, 0.0).astype(F32),
            precision=lax.Precision.HIGHEST, preferred_element_type=F32,
        )
        hot = jnp.where(hot, 1.0, 0.0).astype(BF16)
        apart = lax.broadcasted_iota(jnp.int32, (24, CHUNK), 0) - across
        for a in range(3):
            wide = nn(conv_w[a], hot)
            out = jnp.zeros((24, CHUNK), F32)
            for k in range(3):
                out = jnp.where(apart == k, wide[k : k + 1, :], out)
            own.columns[a] = out
        for half in range(2):

            def pair(p):
                rows = []
                for one in range(2):
                    away = (10 * half + 2 * p + one) - down
                    out = jnp.where(away == 2, own.columns[2], 0.0)
                    out = jnp.where(away == 1, own.columns[1], out)
                    rows.append(jnp.where(away == 0, own.columns[0], out))
                low = pl.multiple_of(p * 48, 48)
                own.t_all[j, half, pl.ds(low, 48), :] = jnp.concatenate(rows, axis=0).astype(BF16)

            loop(0, 5, pair)

    def forward_heads(j):
        own.slope[j] = nn(own.pic_h[...], own.t_all[j, 0]) + own.bias[j]

    def forward(j, heads=None):
        pre1 = nn(own.pic_r[...], own.t_all[j, 1])
        if heads is None:
            pre1 = pre1 + nn(own.pic_h[...], own.t_all[j, 0]) + own.bias[j]
        else:
            pre1 = pre1 + heads[j]
        sigma = 0.5 * jnp.tanh(0.5 * pre1) + 0.5
        act = pre1 * sigma
        own.slope[j] = sigma + act * (1.0 - sigma)
        own.acc[...] += nt(act.astype(BF16), own.w_all[j])

    def backward(j):
        act_grad = nn(own.pre2_grad[...], own.w_all[j])
        pre1_grad = (act_grad * own.slope[j]).astype(BF16)
        own.p1[j] = pre1_grad
        own.grad_r[...] += nt(pre1_grad, own.t_all[j, 1])

    def backward_heads(j):
        own.grad_h[...] += nt(own.p1[j], own.t_all[j, 0])

    def pick_heads(r, table):
        heads = nn(table, hot_rows(head_ids[r : r + 1, :], ENT))
        own.pic_h[...] = nn(heads.T.astype(BF16), space_ref[:D, :]).astype(BF16)

    def pick_relations(r, table):
        relations = nn(table, hot_rows(rel_ids[r : r + 1, :], REL))
        own.pic_r[...] = nn(relations.T.astype(BF16), space_ref[:D, :]).astype(BF16)

    def rows_go(r, table):
        b = rounds[r]
        rows = nn(table, hot_rows(own.negs_in[r, r : r + 1, :], ENT)).T.astype(BF16)
        b.pick_neg[...] = nn(rows, widen()).astype(BF16)
        rows = nn(table, hot_rows(own.tails_in[r, r : r + 1, :], ENT)).T.astype(BF16)
        b.pick_tail[...] = nn(rows, widen()).astype(BF16)
        slot = b.negs.at[c, y_lo, z]
        return (
            [copies.start(b.pick_neg, slot, across[r](i)) for i in zs + [z]],
            copies.start(b.pick_tail, b.tails, partners[r]),
        )

    def negs_beside(r):
        half = rounds[r].negs.at[c, y_lo]
        return copies.start(half, half, beside)

    def negs_to_mate(r):
        half = rounds[r].negs.at[c]
        return copies.start(half, half, mate)

    loop(0, 2, build)
    for pair in asked:
        wait_all(pair)
    table = ent_in[...].astype(BF16)
    along, tail_go = rows_go(0, table)
    pick_heads(0, table)
    pick_relations(0, rel_in[...].astype(BF16))
    loop(2, STEPS, build)
    wait_all(along)
    near = negs_beside(0)
    wait_all(w_copies)
    own.acc[...] = jnp.zeros_like(own.acc)
    loop(0, 5, forward)
    near.wait()
    near = negs_to_mate(0)
    loop(5, STEPS, forward)
    near.wait()
    tail_go.wait()

    for r in range(2):
        b = rounds[r]
        more = r == 0
        if r == 1:
            own.acc[...] = jnp.zeros_like(own.acc)
            loop(0, STEPS, lambda j: forward(j, own.slope))
            near.wait()
            tail_go.wait()
        pre2 = own.acc[...] + fc_bias[...]
        sigma = jax.nn.sigmoid(pre2)
        query = nn((pre2 * sigma).astype(BF16), widen()).astype(BF16)
        tails = b.tails[...].astype(F32)
        wide = query.astype(F32)
        pos_grad = -jax.nn.sigmoid(-jnp.sum(wide * tails, axis=1, keepdims=True))
        negset = b.negs[...].reshape(1024, LANES)
        by_neg = (negative_weight * jax.nn.sigmoid(nt(negset, query))).astype(BF16)
        b.neg_part[...] = nn(by_neg, query).astype(BF16).reshape(2, 2, 8, NEG, LANES)
        b1_copy = copies.start(b.neg_part.at[1 - c], b.b1, mate)
        b.tail_grad[...] = (pos_grad * wide).T[:D]
        tail_copy = copies.start(b.tail_grad, b.tail_in, partners[r])
        by_row = (negative_weight * jax.nn.sigmoid(nt(query, negset))).astype(BF16)
        query_grad = (pos_grad * tails + nn(by_row, negset))[:, :D]
        own.pre2_grad[...] = (query_grad * (sigma * (1.0 + pre2 * (1.0 - sigma)))).astype(BF16)
        own.grad_h[...] = jnp.zeros_like(own.grad_h)
        own.grad_r[...] = jnp.zeros_like(own.grad_r)
        loop(0, 3, backward)
        b1_copy.wait()
        b.b2_send[...] = (b.neg_part[c, 1 - y_lo].astype(F32) + b.b1[1 - y_lo].astype(F32)).astype(BF16)
        b2_copy = copies.start(b.b2_send, b.b2_recv, beside)
        loop(3, STEPS, backward)
        relation_grad = spread_nt_right(own.grad_r[...], space_ref[...])
        rel_row = rel_ids[r : r + 1, :]
        half = REL_PAD // 2

        def part_of(core):
            where = lax.broadcasted_iota(jnp.int32, (half, TRI), 0) + core * half
            hot = jnp.where(where == rel_row, 1.0, 0.0).astype(BF16)
            return spread_dot(hot, relation_grad).reshape(4, 4, BLK, LANES)

        b.s0_send[...] = part_of(1 - c).astype(BF16)
        s0_copy = copies.start(b.s0_send, b.s0_recv, mate)
        own.own_part[...] = part_of(c)
        s0_copy.wait()
        joined = own.own_part[...] + b.s0_recv[...].astype(F32)
        own.own_part[...] = joined
        s1_copies = []
        for h in range(2):
            b.s1_send[h] = joined[..., h * 128 : h * 128 + 128].astype(BF16)
            s1_copies.append(
                [
                    copies.start(b.s1_send.at[h, i, k], b.s1_recv.at[h, d], me.at(x=i, y=k))
                    for d, (i, k) in enumerate(plane)
                ]
            )
        b2_copy.wait()
        b.b3_send[...] = (
            b.neg_part[c, y_lo].astype(F32) + b.b1[y_lo].astype(F32) + b.b2_recv[...].astype(F32)
        ).astype(BF16)
        b3_copies = [
            copies.start(b.b3_send.at[i], b.b3_recv.at[d], me.at(z=i)) for d, i in enumerate(zs)
        ]
        loop(0, STEPS, backward_heads)
        head_grad = spread_nt(space_ref[:D, :], own.grad_h[...])
        own.ent_grad[...] = spread_nt_right(head_grad, hot_rows(head_ids[r : r + 1, :], ENT))
        wait_all(b3_copies)
        share = b.b3_send[z].astype(F32)
        for d in range(7):
            share = share + b.b3_recv[d].astype(F32)
        b.b4_send[...] = share
        b4_copy = copies.start(b.b4_send, b.b4_recv, partners[r])
        z_copies = []
        for h in range(2):
            wait_all(s1_copies[h])
            mine = own.own_part[me.x, me.y][:, h * 128 : h * 128 + 128]
            for d in range(15):
                mine = mine + b.s1_recv[h, d].astype(F32)
            b.z_buf[h, z] = mine.astype(BF16)
            slot = b.z_buf.at[h, z]
            z_copies.append([copies.start(slot, slot, me.at(z=i)) for i in zs])
        tail_copy.wait()
        own.ent_grad[...] += spread_nt_right(b.tail_in[...], hot_rows(own.tails_in[r, r : r + 1, :], ENT))
        b4_copy.wait()
        gradient = own.ent_grad[...] + spread_nt_right(
            b.b4_recv[...].T[:D], hot_rows(own.negs_in[r, r : r + 1, :], ENT)
        )
        if more:
            new_rows, new_state = step_of(ent_in[...], ent_state_in[...], gradient)
        else:
            new_rows, new_state = step_of(ent[...], ent_state[...], gradient)
        ent[...] = new_rows
        ent_state[...] = new_state
        if more:
            table = ent[...].astype(BF16)
            along, tail_go = rows_go(1, table)
            pick_heads(1, table)
        s4_copies = []
        for h in range(2):
            wait_all(z_copies[h])
            total = b.z_buf[h, 0].astype(F32)
            for i in range(1, 8):
                total = total + b.z_buf[h, i].astype(F32)
            b.g_buf[h, c, me.x, me.y] = total.astype(BF16)
            slot = b.g_buf.at[h, c, me.x, me.y]
            s4_copies.append([copies.start(slot, slot, me.at(x=i, y=k)) for i, k in plane])
        if more:
            loop(0, STEPS, forward_heads)
            wait_all(along)
            near = negs_beside(1)
        s6_copies = []
        for h in range(2):
            wait_all(s4_copies[h])
            slot = b.g_buf.at[h, c]
            s6_copies.append(copies.start(slot, slot, mate))
        if more:
            near.wait()
            near = negs_to_mate(1)
        wait_all(s6_copies)
        wide = widen()
        gradient = (
            nt(wide[:, :128], b.g_buf[0].reshape(REL_PAD, 128)) + nt(wide[:, 128:], b.g_buf[1].reshape(REL_PAD, 128))
        )[:, :REL]
        if more:
            new_rows, new_state = step_of(rel_in[...], rel_state_in[...].reshape(1, REL), gradient)
        else:
            new_rows, new_state = step_of(rel[...], rel_state[...].reshape(1, REL), gradient)
        rel[...] = new_rows
        rel_state[...] = new_state.reshape(REL)
        if more:
            pick_relations(1, new_rows.astype(BF16))


def shards(
    entity_rows, entity_state, relation_rows, relation_state,
    conv_weight, conv_bias, fc_weight, fc_bias,
    head_ids, rel_ids, tail_ids, neg_ids,
):
    vmem = pl.BlockSpec(memory_space=pltpu.VMEM)
    operands = [
        head_ids, rel_ids, tail_ids, neg_ids,
        entity_rows.T, entity_state.reshape(1, ENT), relation_rows.T, relation_state,
        jnp.transpose(conv_weight, (1, 2, 0)), conv_bias.reshape(1, FILTERS),
        fc_weight.T, fc_bias.reshape(1, D), features(), spacing(),
    ]
    specs = [vmem] * len(operands)
    specs[10] = pl.BlockSpec(memory_space=pl.ANY)
    ent, ent_state, rel, rel_state = pl.pallas_call(
        window_kernel,
        out_shape=(
            jax.ShapeDtypeStruct((D, ENT), F32),
            jax.ShapeDtypeStruct((1, ENT), F32),
            jax.ShapeDtypeStruct((D, REL), F32),
            jax.ShapeDtypeStruct((REL,), F32),
        ),
        in_specs=specs,
        out_specs=(vmem,) * 4,
        scratch_shapes=[
            *SHARED_SCRATCH.values(),
            *ROUND_SCRATCH.values(),
            *ROUND_SCRATCH.values(),
            pltpu.SemaphoreType.DMA((STEPS,)),
            pltpu.SemaphoreType.DMA((COPIES,)),
            pltpu.SemaphoreType.DMA((COPIES,)),
        ],
        compiler_params=pltpu.CompilerParams(
            collective_id=0, has_side_effects=True, vmem_limit_bytes=60 << 20
        ),
        name="window",
    )(*operands)
    return ent.T, ent_state.reshape(ENT), rel.T, rel_state


def solution(mesh):
    both = ("group", "shard")
    in_specs = (
        P(both, None), P(both), P(), P(), P(), P(), P(), P(),
        P(None, both), P(None, both), P(None, both), P(None, both),
    )
    out_specs = (P(both, None), P(both), P(), P())
    return jax.shard_map(shards, mesh=mesh, in_specs=in_specs, out_specs=out_specs, check_vma=False)
```

```python
import jax
import jax.numpy as jnp
import numpy as np
from jax import lax
from jax.experimental import pallas as pl
from jax.experimental.pallas import tpu as pltpu
from jax.sharding import PartitionSpec as P

D = 200
FILTERS = 32
FLAT = 10368
REL = 1387
REL_PAD = 1536
BLK = 48
TRI = 128
NEG = 32
ENT = 1024
CHUNK = 1152
STEPS = FLAT // CHUNK
WIDE = 240
LANES = 256
MESH = pl.DeviceIdType.MESH
F32 = jnp.float32
BF16 = jnp.bfloat16

negative_weight = 0.03125
learn_rate = 0.5

NT = (((1,), (1,)), ((), ()))


def nn(a, b):
    return jnp.dot(a, b, preferred_element_type=F32)


def nt(a, b):
    return lax.dot_general(a, b, NT, preferred_element_type=F32)


def spread_dot(one_hot, values):
    high = values.astype(BF16)
    low = (values - high.astype(F32)).astype(BF16)
    return nn(one_hot, high) + nn(one_hot, low)


def hot_rows(ids_row, extent):
    where = lax.broadcasted_iota(jnp.int32, (extent, ids_row.shape[1]), 0)
    return jnp.where(where == ids_row, 1.0, 0.0).astype(BF16)


class Place:
    def __init__(self):
        group = lax.axis_index("group")
        shard = lax.axis_index("shard")
        self.x = group % 4
        self.y_hi = group // 4
        self.y_lo = shard // 16
        self.z = (shard // 2) % 8
        self.core = shard % 2
        self.y = self.y_hi * 2 + self.y_lo

    def at(self, x=None, y=None, z=None, core=None):
        x = self.x if x is None else x
        y = self.y if y is None else y
        z = self.z if z is None else z
        core = self.core if core is None else core
        return ((y // 2) * 4 + x, (y % 2) * 16 + z * 2 + core)

    def mate(self):
        return self.at(core=1 - self.core)

    def beside(self):
        return self.at(y=self.y_hi * 2 + 1 - self.y_lo)

    def partner(self, bit):
        if bit == 0:
            return self.at(x=self.x + 1 - 2 * (self.x % 2))
        return self.at(x=(self.x + 2) % 4)


class Copies:
    def __init__(self, send, recv):
        self.send, self.recv, self.used = send, recv, 0

    def start(self, src, dst, device):
        copy = pltpu.make_async_remote_copy(
            src_ref=src,
            dst_ref=dst,
            send_sem=self.send.at[self.used],
            recv_sem=self.recv.at[self.used],
            device_id=device,
            device_id_type=MESH,
        )
        self.used += 1
        copy.start()
        return copy


def greet(peers):
    barrier = pltpu.get_barrier_semaphore()
    for peer in peers:
        pl.semaphore_signal(barrier, inc=1, device_id=peer, device_id_type=MESH)
    return lambda: pl.semaphore_wait(barrier, len(peers))


def wait_all(copies):
    for copy in copies:
        copy.wait()


def spacing():
    d = np.arange(D)
    out = np.zeros((LANES, WIDE), np.float32)
    out[d, d // 20 * 24 + d % 20] = 1.0
    return jnp.asarray(out, BF16)


def features():
    q = np.arange(FLAT).reshape(STEPS, 1, CHUNK)
    return jnp.asarray(np.concatenate([q % 324 // 18, q % 18, q // 324], axis=1).astype(np.int32))


def spread_nt(one_hot, values):
    high = values.astype(BF16)
    low = (values - high.astype(F32)).astype(BF16)
    return nt(one_hot, high) + nt(one_hot, low)


def spread_nt_right(values, one_hot):
    high = values.astype(BF16)
    low = (values - high.astype(F32)).astype(BF16)
    return nt(high, one_hot) + nt(low, one_hot)


def step_of(rows, state, gradient):
    state = state + jnp.sum(gradient * gradient, axis=0, keepdims=True) * (1.0 / D)
    return rows - learn_rate * gradient * lax.rsqrt(state), state


def widen():
    row = lax.broadcasted_iota(jnp.int32, (D, LANES), 0)
    return jnp.where(row == lax.broadcasted_iota(jnp.int32, (D, LANES), 1), 1.0, 0.0).astype(BF16)


def loop(first, last, body):
    def one(j, carry):
        body(j)
        return carry

    lax.fori_loop(first, last, one, 0)


ROUND_SCRATCH = dict(
    tails=pltpu.VMEM((TRI, LANES), BF16),
    negs=pltpu.VMEM((2, 2, 8, NEG, LANES), BF16),
    pick_tail=pltpu.VMEM((TRI, LANES), BF16),
    pick_neg=pltpu.VMEM((NEG, LANES), BF16),
    neg_part=pltpu.VMEM((2, 2, 8, NEG, LANES), BF16),
    tail_grad=pltpu.VMEM((D, TRI), F32),
    tail_in=pltpu.VMEM((D, TRI), F32),
    b1=pltpu.VMEM((2, 8, NEG, LANES), BF16),
    b2_send=pltpu.VMEM((8, NEG, LANES), BF16),
    b2_recv=pltpu.VMEM((8, NEG, LANES), BF16),
    b3_send=pltpu.VMEM((8, NEG, LANES), BF16),
    b3_recv=pltpu.VMEM((7, NEG, LANES), BF16),
    b4_send=pltpu.VMEM((NEG, LANES), F32),
    b4_recv=pltpu.VMEM((NEG, LANES), F32),
    s0_send=pltpu.VMEM((4, 4, BLK, LANES), BF16),
    s0_recv=pltpu.VMEM((4, 4, BLK, LANES), BF16),
    s1_send=pltpu.VMEM((2, 4, 4, BLK, 128), BF16),
    s1_recv=pltpu.VMEM((2, 15, BLK, 128), BF16),
    z_buf=pltpu.VMEM((2, 8, BLK, 128), BF16),
    g_buf=pltpu.VMEM((2, 2, 4, 4, BLK, 128), BF16),
)
SHARED_SCRATCH = dict(
    tails_in=pltpu.VMEM((2, 2, TRI), jnp.int32),
    negs_in=pltpu.VMEM((2, 2, NEG), jnp.int32),
    columns=pltpu.VMEM((3, 24, CHUNK), F32),
    t_all=pltpu.VMEM((STEPS, 2, WIDE, CHUNK), BF16),
    w_all=pltpu.VMEM((STEPS, D, CHUNK), BF16),
    p1=pltpu.VMEM((STEPS, TRI, CHUNK), BF16),
    bias=pltpu.VMEM((STEPS, 1, CHUNK), F32),
    slope=pltpu.VMEM((STEPS, TRI, CHUNK), F32),
    pic_h=pltpu.VMEM((TRI, WIDE), BF16),
    pic_r=pltpu.VMEM((TRI, WIDE), BF16),
    acc=pltpu.VMEM((TRI, D), F32),
    grad_h=pltpu.VMEM((TRI, WIDE), F32),
    grad_r=pltpu.VMEM((TRI, WIDE), F32),
    pre2_grad=pltpu.VMEM((TRI, D), BF16),
    own_part=pltpu.VMEM((4, 4, BLK, LANES), F32),
    ent_grad=pltpu.VMEM((D, ENT), F32),
    ent=pltpu.VMEM((D, ENT), F32),
    rel=pltpu.VMEM((D, REL), F32),
)
COPIES = 4 + 2 * (1 + 8 + 1 + 1) + 2 * (1 + 1 + 1 + 7 + 1 + 1 + 2 * (15 + 7 + 15 + 1))


class Bag:
    def __init__(self, names, refs):
        self.__dict__.update(zip(names, refs))


def window_kernel(
    head_ids, rel_ids, tail_ids, neg_ids, ent_hbm, ent_state_in, rel_hbm, rel_state_in,
    conv_w, conv_b, w_hbm, fc_bias, place_ref, space_ref,
    ent_out, ent_state, rel, rel_state, *rest,
):
    own = Bag(SHARED_SCRATCH, rest)
    rest = rest[len(SHARED_SCRATCH):]
    rounds = []
    for r in range(2):
        rounds.append(Bag(ROUND_SCRATCH, rest))
        rest = rest[len(ROUND_SCRATCH):]
    w_sem, send, recv = rest
    me = Place()
    copies = Copies(send, recv)
    c, z, y_lo = me.core, me.z, me.y_lo
    steps = sorted(
        ((dx, dy) for dx in range(4) for dy in range(4) if dx or dy),
        key=lambda d: -min(d[0], 4 - d[0]) - min(d[1], 4 - d[1]),
    )
    plane = [((me.x + dx) % 4, (me.y + dy) % 4) for dx, dy in steps]
    zs = [(z + d) % 8 for d in range(1, 8)]
    mate, beside = me.mate(), me.beside()
    partners = [me.partner(0), me.partner(1)]
    across = [
        lambda i: me.at(x=me.x + 1 - 2 * (me.x % 2), z=i),
        lambda i: me.at(x=(me.x + 2) % 4, z=i),
    ]

    peers = (
        [mate]
        + [me.at(x=i, y=k) for i, k in plane]
        + [me.at(z=i) for i in zs]
        + [at(i) for at in across for i in zs]
    )
    all_here = greet(peers)
    ent_copy = pltpu.make_async_copy(ent_hbm, own.ent, w_sem.at[STEPS])
    rel_copy = pltpu.make_async_copy(rel_hbm, own.rel, w_sem.at[STEPS + 1])
    ent_copy.start()
    rel_copy.start()
    w_copies = []
    for j in range(STEPS):
        copy = pltpu.make_async_copy(
            w_hbm.at[:, pl.ds(j * CHUNK, CHUNK)], own.w_all.at[j], w_sem.at[j]
        )
        copy.start()
        w_copies.append(copy)
    def build(j):
        down, across, filt = (place_ref[j, k : k + 1, :] for k in range(3))
        hot = lax.broadcasted_iota(jnp.int32, (FILTERS, CHUNK), 0) == filt
        own.bias[j] = jnp.dot(
            conv_b[...], jnp.where(hot, 1.0, 0.0).astype(F32),
            precision=lax.Precision.HIGHEST, preferred_element_type=F32,
        )
        hot = jnp.where(hot, 1.0, 0.0).astype(BF16)
        apart = lax.broadcasted_iota(jnp.int32, (24, CHUNK), 0) - across
        for a in range(3):
            wide = nn(conv_w[a], hot)
            out = jnp.zeros((24, CHUNK), F32)
            for k in range(3):
                out = jnp.where(apart == k, wide[k : k + 1, :], out)
            own.columns[a] = out
        for half in range(2):

            def pair(p):
                rows = []
                for one in range(2):
                    away = (10 * half + 2 * p + one) - down
                    out = jnp.where(away == 2, own.columns[2], 0.0)
                    out = jnp.where(away == 1, own.columns[1], out)
                    rows.append(jnp.where(away == 0, own.columns[0], out))
                low = pl.multiple_of(p * 48, 48)
                own.t_all[j, half, pl.ds(low, 48), :] = jnp.concatenate(rows, axis=0).astype(BF16)

            loop(0, 5, pair)

    def forward_heads(j):
        own.slope[j] = nn(own.pic_h[...], own.t_all[j, 0]) + own.bias[j]

    def forward(j, heads=None):
        pre1 = nn(own.pic_r[...], own.t_all[j, 1])
        if heads is None:
            pre1 = pre1 + nn(own.pic_h[...], own.t_all[j, 0]) + own.bias[j]
        else:
            pre1 = pre1 + heads[j]
        sigma = 0.5 * jnp.tanh(0.5 * pre1) + 0.5
        act = pre1 * sigma
        own.slope[j] = sigma + act * (1.0 - sigma)
        own.acc[...] += nt(act.astype(BF16), own.w_all[j])

    def backward(j):
        act_grad = nn(own.pre2_grad[...], own.w_all[j])
        pre1_grad = (act_grad * own.slope[j]).astype(BF16)
        own.p1[j] = pre1_grad
        own.grad_r[...] += nt(pre1_grad, own.t_all[j, 1])

    def backward_heads(j):
        own.grad_h[...] += nt(own.p1[j], own.t_all[j, 0])

    def pick_heads(r, table):
        heads = nn(table, hot_rows(head_ids[r : r + 1, :], ENT))
        own.pic_h[...] = nn(heads.T.astype(BF16), space_ref[:D, :]).astype(BF16)

    def pick_relations(r, table):
        relations = nn(table, hot_rows(rel_ids[r : r + 1, :], REL))
        own.pic_r[...] = nn(relations.T.astype(BF16), space_ref[:D, :]).astype(BF16)

    def rows_go(r, table):
        b = rounds[r]
        rows = nn(table, hot_rows(own.negs_in[r, r : r + 1, :], ENT)).T.astype(BF16)
        b.pick_neg[...] = nn(rows, widen()).astype(BF16)
        rows = nn(table, hot_rows(own.tails_in[r, r : r + 1, :], ENT)).T.astype(BF16)
        b.pick_tail[...] = nn(rows, widen()).astype(BF16)
        slot = b.negs.at[c, y_lo, z]
        return (
            [copies.start(b.pick_neg, slot, across[r](i)) for i in zs + [z]],
            copies.start(b.pick_tail, b.tails, partners[r]),
        )

    def negs_beside(r):
        half = rounds[r].negs.at[c, y_lo]
        return copies.start(half, half, beside)

    def negs_to_mate(r):
        half = rounds[r].negs.at[c]
        return copies.start(half, half, mate)

    loop(0, 4, build)
    all_here()
    asked = [
        (
            copies.start(tail_ids, own.tails_in.at[r], partners[r]),
            copies.start(neg_ids, own.negs_in.at[r], partners[r]),
        )
        for r in range(2)
    ]
    ent_copy.wait()
    table = own.ent[...].astype(BF16)
    pick_heads(0, table)
    loop(4, 7, build)
    for pair in asked:
        wait_all(pair)
    along, tail_go = rows_go(0, table)
    loop(7, STEPS, build)
    rel_copy.wait()
    pick_relations(0, own.rel[...].astype(BF16))
    wait_all(w_copies)
    own.acc[...] = jnp.zeros_like(own.acc)
    loop(0, 5, forward)
    wait_all(along)
    near = negs_beside(0)
    loop(5, STEPS, forward)
    near.wait()
    near = negs_to_mate(0)
    near.wait()
    tail_go.wait()

    for r in range(2):
        b = rounds[r]
        more = r == 0
        if r == 1:
            own.acc[...] = jnp.zeros_like(own.acc)
            loop(0, STEPS, lambda j: forward(j, own.slope))
            near.wait()
            tail_go.wait()
        pre2 = own.acc[...] + fc_bias[...]
        sigma = jax.nn.sigmoid(pre2)
        query = nn((pre2 * sigma).astype(BF16), widen()).astype(BF16)
        tails = b.tails[...].astype(F32)
        wide = query.astype(F32)
        pos_grad = -jax.nn.sigmoid(-jnp.sum(wide * tails, axis=1, keepdims=True))
        negset = b.negs[...].reshape(1024, LANES)
        by_neg = (negative_weight * jax.nn.sigmoid(nt(negset, query))).astype(BF16)
        b.neg_part[...] = nn(by_neg, query).astype(BF16).reshape(2, 2, 8, NEG, LANES)
        b1_copy = copies.start(b.neg_part.at[1 - c], b.b1, mate)
        b.tail_grad[...] = (pos_grad * wide).T[:D]
        tail_copy = copies.start(b.tail_grad, b.tail_in, partners[r])
        by_row = (negative_weight * jax.nn.sigmoid(nt(query, negset))).astype(BF16)
        query_grad = (pos_grad * tails + nn(by_row, negset))[:, :D]
        own.pre2_grad[...] = (query_grad * (sigma * (1.0 + pre2 * (1.0 - sigma)))).astype(BF16)
        own.grad_h[...] = jnp.zeros_like(own.grad_h)
        own.grad_r[...] = jnp.zeros_like(own.grad_r)
        loop(0, 3, backward)
        b1_copy.wait()
        b.b2_send[...] = (b.neg_part[c, 1 - y_lo].astype(F32) + b.b1[1 - y_lo].astype(F32)).astype(BF16)
        b2_copy = copies.start(b.b2_send, b.b2_recv, beside)
        loop(3, STEPS, backward)
        relation_grad = spread_nt_right(own.grad_r[...], space_ref[...])
        rel_row = rel_ids[r : r + 1, :]
        half = REL_PAD // 2

        def part_of(core):
            where = lax.broadcasted_iota(jnp.int32, (half, TRI), 0) + core * half
            hot = jnp.where(where == rel_row, 1.0, 0.0).astype(BF16)
            return spread_dot(hot, relation_grad).reshape(4, 4, BLK, LANES)

        b.s0_send[...] = part_of(1 - c).astype(BF16)
        s0_copy = copies.start(b.s0_send, b.s0_recv, mate)
        own.own_part[...] = part_of(c)
        s0_copy.wait()
        joined = own.own_part[...] + b.s0_recv[...].astype(F32)
        own.own_part[...] = joined
        s1_copies = []
        for h in range(2):
            b.s1_send[h] = joined[..., h * 128 : h * 128 + 128].astype(BF16)
            s1_copies.append(
                [
                    copies.start(b.s1_send.at[h, i, k], b.s1_recv.at[h, d], me.at(x=i, y=k))
                    for d, (i, k) in enumerate(plane)
                ]
            )
        b2_copy.wait()
        b.b3_send[...] = (
            b.neg_part[c, y_lo].astype(F32) + b.b1[y_lo].astype(F32) + b.b2_recv[...].astype(F32)
        ).astype(BF16)
        b3_copies = [
            copies.start(b.b3_send.at[i], b.b3_recv.at[d], me.at(z=i)) for d, i in enumerate(zs)
        ]
        loop(0, STEPS, backward_heads)
        head_grad = spread_nt(space_ref[:D, :], own.grad_h[...])
        own.ent_grad[...] = spread_nt_right(head_grad, hot_rows(head_ids[r : r + 1, :], ENT))
        wait_all(b3_copies)
        share = b.b3_send[z].astype(F32)
        for d in range(7):
            share = share + b.b3_recv[d].astype(F32)
        b.b4_send[...] = share
        b4_copy = copies.start(b.b4_send, b.b4_recv, partners[r])
        z_copies = []
        for h in range(2):
            wait_all(s1_copies[h])
            mine = own.own_part[me.x, me.y][:, h * 128 : h * 128 + 128]
            for d in range(15):
                mine = mine + b.s1_recv[h, d].astype(F32)
            b.z_buf[h, z] = mine.astype(BF16)
            slot = b.z_buf.at[h, z]
            z_copies.append([copies.start(slot, slot, me.at(z=i)) for i in zs])
        tail_copy.wait()
        own.ent_grad[...] += spread_nt_right(b.tail_in[...], hot_rows(own.tails_in[r, r : r + 1, :], ENT))
        b4_copy.wait()
        gradient = own.ent_grad[...] + spread_nt_right(
            b.b4_recv[...].T[:D], hot_rows(own.negs_in[r, r : r + 1, :], ENT)
        )
        new_rows, new_state = step_of(own.ent[...], (ent_state_in if more else ent_state)[...], gradient)
        own.ent[...] = new_rows
        ent_state[...] = new_state
        if not more:
            ent_copy = pltpu.make_async_copy(own.ent, ent_out, w_sem.at[STEPS])
            ent_copy.start()
        if more:
            table = own.ent[...].astype(BF16)
            along, tail_go = rows_go(1, table)
            pick_heads(1, table)
        s4_copies = []
        for h in range(2):
            wait_all(z_copies[h])
            total = b.z_buf[h, 0].astype(F32)
            for i in range(1, 8):
                total = total + b.z_buf[h, i].astype(F32)
            b.g_buf[h, c, me.x, me.y] = total.astype(BF16)
            slot = b.g_buf.at[h, c, me.x, me.y]
            s4_copies.append([copies.start(slot, slot, me.at(x=i, y=k)) for i, k in plane])
        if more:
            loop(0, STEPS, forward_heads)
            wait_all(along)
            near = negs_beside(1)
        s6_copies = []
        for h in range(2):
            wait_all(s4_copies[h])
            slot = b.g_buf.at[h, c]
            s6_copies.append(copies.start(slot, slot, mate))
        if more:
            near.wait()
            near = negs_to_mate(1)
        wait_all(s6_copies)
        wide = widen()
        gradient = (
            nt(wide[:, :128], b.g_buf[0].reshape(REL_PAD, 128)) + nt(wide[:, 128:], b.g_buf[1].reshape(REL_PAD, 128))
        )[:, :REL]
        old_state = (rel_state_in if more else rel_state)[...].reshape(1, REL)
        new_rows, new_state = step_of(own.rel[...], old_state, gradient)
        if more:
            own.rel[...] = new_rows
        else:
            rel[...] = new_rows
            ent_copy.wait()
        rel_state[...] = new_state.reshape(REL)
        if more:
            pick_relations(1, new_rows.astype(BF16))


def shards(
    entity_rows, entity_state, relation_rows, relation_state,
    conv_weight, conv_bias, fc_weight, fc_bias,
    head_ids, rel_ids, tail_ids, neg_ids,
):
    vmem = pl.BlockSpec(memory_space=pltpu.VMEM)
    operands = [
        head_ids, rel_ids, tail_ids, neg_ids,
        entity_rows.T, entity_state.reshape(1, ENT), relation_rows.T, relation_state,
        jnp.transpose(conv_weight, (1, 2, 0)), conv_bias.reshape(1, FILTERS),
        fc_weight.T, fc_bias.reshape(1, D), features(), spacing(),
    ]
    specs = [vmem] * len(operands)
    far = pl.BlockSpec(memory_space=pltpu.HBM)
    specs[4] = specs[6] = specs[10] = far
    ent, ent_state, rel, rel_state = pl.pallas_call(
        window_kernel,
        out_shape=(
            jax.ShapeDtypeStruct((D, ENT), F32),
            jax.ShapeDtypeStruct((1, ENT), F32),
            jax.ShapeDtypeStruct((D, REL), F32),
            jax.ShapeDtypeStruct((REL,), F32),
        ),
        in_specs=specs,
        out_specs=(far, vmem, vmem, vmem),
        scratch_shapes=[
            *SHARED_SCRATCH.values(),
            *ROUND_SCRATCH.values(),
            *ROUND_SCRATCH.values(),
            pltpu.SemaphoreType.DMA((STEPS + 2,)),
            pltpu.SemaphoreType.DMA((COPIES,)),
            pltpu.SemaphoreType.DMA((COPIES,)),
        ],
        compiler_params=pltpu.CompilerParams(
            collective_id=0, has_side_effects=True, vmem_limit_bytes=60 << 20
        ),
        name="window",
    )(*operands)
    return ent.T, ent_state.reshape(ENT), rel.T, rel_state


def solution(mesh):
    both = ("group", "shard")
    in_specs = (
        P(both, None), P(both), P(), P(), P(), P(), P(), P(),
        P(None, both), P(None, both), P(None, both), P(None, both),
    )
    out_specs = (P(both, None), P(both), P(), P())
    return jax.shard_map(shards, mesh=mesh, in_specs=in_specs, out_specs=out_specs, check_vma=False)
```

```python
import jax
import jax.numpy as jnp
import numpy as np
from jax import lax
from jax.experimental import pallas as pl
from jax.experimental.pallas import tpu as pltpu
from jax.sharding import PartitionSpec as P

D = 200
FILTERS = 32
FLAT = 10368
REL = 1387
REL_PAD = 1536
BLK = 48
TRI = 128
NEG = 32
ENT = 1024
CHUNK = 1152
STEPS = FLAT // CHUNK
WIDE = 240
LANES = 256
MESH = pl.DeviceIdType.MESH
F32 = jnp.float32
BF16 = jnp.bfloat16

negative_weight = 0.03125
learn_rate = 0.5

NT = (((1,), (1,)), ((), ()))


def nn(a, b):
    return jnp.dot(a, b, preferred_element_type=F32)


def nt(a, b):
    return lax.dot_general(a, b, NT, preferred_element_type=F32)


def spread_dot(one_hot, values):
    high = values.astype(BF16)
    low = (values - high.astype(F32)).astype(BF16)
    return nn(one_hot, high) + nn(one_hot, low)


def hot_rows(ids_row, extent):
    where = lax.broadcasted_iota(jnp.int32, (extent, ids_row.shape[1]), 0)
    return jnp.where(where == ids_row, 1.0, 0.0).astype(BF16)


class Place:
    def __init__(self):
        group = lax.axis_index("group")
        shard = lax.axis_index("shard")
        self.x = group % 4
        self.y_hi = group // 4
        self.y_lo = shard // 16
        self.z = (shard // 2) % 8
        self.core = shard % 2
        self.y = self.y_hi * 2 + self.y_lo

    def at(self, x=None, y=None, z=None, core=None):
        x = self.x if x is None else x
        y = self.y if y is None else y
        z = self.z if z is None else z
        core = self.core if core is None else core
        return ((y // 2) * 4 + x, (y % 2) * 16 + z * 2 + core)

    def mate(self):
        return self.at(core=1 - self.core)

    def beside(self):
        return self.at(y=self.y_hi * 2 + 1 - self.y_lo)

    def partner(self, bit):
        if bit == 0:
            return self.at(x=self.x + 1 - 2 * (self.x % 2))
        return self.at(x=(self.x + 2) % 4)


class Copies:
    def __init__(self, send, recv):
        self.send, self.recv, self.used = send, recv, 0

    def start(self, src, dst, device):
        copy = pltpu.make_async_remote_copy(
            src_ref=src,
            dst_ref=dst,
            send_sem=self.send.at[self.used],
            recv_sem=self.recv.at[self.used],
            device_id=device,
            device_id_type=MESH,
        )
        self.used += 1
        copy.start()
        return copy


def greet(peers):
    barrier = pltpu.get_barrier_semaphore()
    for peer in peers:
        pl.semaphore_signal(barrier, inc=1, device_id=peer, device_id_type=MESH)
    return lambda: pl.semaphore_wait(barrier, len(peers))


def wait_all(copies):
    for copy in copies:
        copy.wait()


def spacing():
    d = np.arange(D)
    out = np.zeros((LANES, WIDE), np.float32)
    out[d, d // 20 * 24 + d % 20] = 1.0
    return jnp.asarray(out, BF16)


def features():
    q = np.arange(FLAT).reshape(STEPS, 1, CHUNK)
    return jnp.asarray(np.concatenate([q % 324 // 18, q % 18, q // 324], axis=1).astype(np.int32))


def spread_nt(one_hot, values):
    high = values.astype(BF16)
    low = (values - high.astype(F32)).astype(BF16)
    return nt(one_hot, high) + nt(one_hot, low)


def spread_nt_right(values, one_hot):
    high = values.astype(BF16)
    low = (values - high.astype(F32)).astype(BF16)
    return nt(high, one_hot) + nt(low, one_hot)


def step_of(rows, state, gradient):
    state = state + jnp.sum(gradient * gradient, axis=0, keepdims=True) * (1.0 / D)
    return rows - learn_rate * gradient * lax.rsqrt(state), state


def widen():
    row = lax.broadcasted_iota(jnp.int32, (D, LANES), 0)
    return jnp.where(row == lax.broadcasted_iota(jnp.int32, (D, LANES), 1), 1.0, 0.0).astype(BF16)


def triples(first, last, body):
    def three(j):
        for k in range(3):
            body(first + 3 * j + k)

    loop(0, (last - first) // 3, three)


def loop(first, last, body):
    def one(j, carry):
        body(j)
        return carry

    lax.fori_loop(first, last, one, 0)


ROUND_SCRATCH = dict(
    tails=pltpu.VMEM((TRI, LANES), BF16),
    negs=pltpu.VMEM((2, 2, 8, NEG, LANES), BF16),
    pick_tail=pltpu.VMEM((TRI, LANES), BF16),
    pick_neg=pltpu.VMEM((NEG, LANES), BF16),
    neg_part=pltpu.VMEM((2, 2, 8, NEG, LANES), BF16),
    tail_grad=pltpu.VMEM((D, TRI), F32),
    tail_in=pltpu.VMEM((D, TRI), F32),
    b1=pltpu.VMEM((2, 8, NEG, LANES), BF16),
    b2_send=pltpu.VMEM((8, NEG, LANES), BF16),
    b2_recv=pltpu.VMEM((8, NEG, LANES), BF16),
    b3_send=pltpu.VMEM((8, NEG, LANES), BF16),
    b3_recv=pltpu.VMEM((7, NEG, LANES), BF16),
    b4_send=pltpu.VMEM((NEG, LANES), F32),
    b4_recv=pltpu.VMEM((NEG, LANES), F32),
    s0_send=pltpu.VMEM((4, 4, BLK, LANES), BF16),
    s0_recv=pltpu.VMEM((4, 4, BLK, LANES), BF16),
    s1_send=pltpu.VMEM((2, 4, 4, BLK, 128), BF16),
    s1_recv=pltpu.VMEM((2, 15, BLK, 128), BF16),
    z_buf=pltpu.VMEM((2, 8, BLK, 128), BF16),
    g_buf=pltpu.VMEM((2, 2, 4, 4, BLK, 128), BF16),
)
SHARED_SCRATCH = dict(
    tails_in=pltpu.VMEM((2, 2, TRI), jnp.int32),
    negs_in=pltpu.VMEM((2, 2, NEG), jnp.int32),
    columns=pltpu.VMEM((3, 24, CHUNK), F32),
    t_all=pltpu.VMEM((STEPS, 2, WIDE, CHUNK), BF16),
    w_all=pltpu.VMEM((STEPS, D, CHUNK), BF16),
    p1=pltpu.VMEM((STEPS, TRI, CHUNK), BF16),
    bias=pltpu.VMEM((STEPS, 1, CHUNK), F32),
    slope=pltpu.VMEM((STEPS, TRI, CHUNK), F32),
    pic_h=pltpu.VMEM((TRI, WIDE), BF16),
    pic_r=pltpu.VMEM((TRI, WIDE), BF16),
    acc=pltpu.VMEM((TRI, D), F32),
    grad_h=pltpu.VMEM((TRI, WIDE), F32),
    grad_r=pltpu.VMEM((TRI, WIDE), F32),
    pre2_grad=pltpu.VMEM((TRI, D), BF16),
    own_part=pltpu.VMEM((4, 4, BLK, LANES), F32),
    ent_grad=pltpu.VMEM((D, ENT), F32),
    ent=pltpu.VMEM((D, ENT), F32),
    rel=pltpu.VMEM((D, REL), F32),
)
COPIES = 4 + 2 * (1 + 8 + 1 + 1) + 2 * (1 + 1 + 1 + 7 + 1 + 1 + 2 * (15 + 7 + 15 + 1))


class Bag:
    def __init__(self, names, refs):
        self.__dict__.update(zip(names, refs))


def window_kernel(
    head_ids, rel_ids, tail_ids, neg_ids, ent_hbm, ent_state_in, rel_hbm, rel_state_in,
    conv_w, conv_b, w_hbm, fc_bias, place_ref, space_ref,
    ent_out, ent_state, rel, rel_state, *rest,
):
    own = Bag(SHARED_SCRATCH, rest)
    rest = rest[len(SHARED_SCRATCH):]
    rounds = []
    for r in range(2):
        rounds.append(Bag(ROUND_SCRATCH, rest))
        rest = rest[len(ROUND_SCRATCH):]
    w_sem, send, recv = rest
    me = Place()
    copies = Copies(send, recv)
    c, z, y_lo = me.core, me.z, me.y_lo
    steps = sorted(
        ((dx, dy) for dx in range(4) for dy in range(4) if dx or dy),
        key=lambda d: -min(d[0], 4 - d[0]) - min(d[1], 4 - d[1]),
    )
    plane = [((me.x + dx) % 4, (me.y + dy) % 4) for dx, dy in steps]
    zs = [(z + d) % 8 for d in range(1, 8)]
    mate, beside = me.mate(), me.beside()
    partners = [me.partner(0), me.partner(1)]
    across = [
        lambda i: me.at(x=me.x + 1 - 2 * (me.x % 2), z=i),
        lambda i: me.at(x=(me.x + 2) % 4, z=i),
    ]

    peers = (
        [mate]
        + [me.at(x=i, y=k) for i, k in plane]
        + [me.at(z=i) for i in zs]
        + [at(i) for at in across for i in zs]
    )
    all_here = greet(peers)
    ent_copy = pltpu.make_async_copy(ent_hbm, own.ent, w_sem.at[STEPS])
    rel_copy = pltpu.make_async_copy(rel_hbm, own.rel, w_sem.at[STEPS + 1])
    ent_copy.start()
    rel_copy.start()
    w_copies = []
    for j in range(STEPS):
        copy = pltpu.make_async_copy(
            w_hbm.at[:, pl.ds(j * CHUNK, CHUNK)], own.w_all.at[j], w_sem.at[j]
        )
        copy.start()
        w_copies.append(copy)
    def build(j):
        down, across, filt = (place_ref[j, k : k + 1, :] for k in range(3))
        hot = lax.broadcasted_iota(jnp.int32, (FILTERS, CHUNK), 0) == filt
        own.bias[j] = jnp.dot(
            conv_b[...], jnp.where(hot, 1.0, 0.0).astype(F32),
            precision=lax.Precision.HIGHEST, preferred_element_type=F32,
        )
        hot = jnp.where(hot, 1.0, 0.0).astype(BF16)
        apart = lax.broadcasted_iota(jnp.int32, (24, CHUNK), 0) - across
        for a in range(3):
            wide = nn(conv_w[a], hot)
            out = jnp.zeros((24, CHUNK), F32)
            for k in range(3):
                out = jnp.where(apart == k, wide[k : k + 1, :], out)
            own.columns[a] = out
        for half in range(2):

            def pair(p):
                rows = []
                for one in range(2):
                    away = (10 * half + 2 * p + one) - down
                    out = jnp.where(away == 2, own.columns[2], 0.0)
                    out = jnp.where(away == 1, own.columns[1], out)
                    rows.append(jnp.where(away == 0, own.columns[0], out))
                low = pl.multiple_of(p * 48, 48)
                own.t_all[j, half, pl.ds(low, 48), :] = jnp.concatenate(rows, axis=0).astype(BF16)

            loop(0, 5, pair)

    def forward_heads(j):
        own.slope[j] = nn(own.pic_h[...], own.t_all[j, 0]) + own.bias[j]

    def forward(j, heads=None):
        pre1 = nn(own.pic_r[...], own.t_all[j, 1])
        if heads is None:
            pre1 = pre1 + nn(own.pic_h[...], own.t_all[j, 0]) + own.bias[j]
        else:
            pre1 = pre1 + heads[j]
        sigma = 0.5 * jnp.tanh(0.5 * pre1) + 0.5
        act = pre1 * sigma
        own.slope[j] = sigma + act * (1.0 - sigma)
        own.acc[...] += nt(act.astype(BF16), own.w_all[j])

    def backward(j):
        act_grad = nn(own.pre2_grad[...], own.w_all[j])
        pre1_grad = (act_grad * own.slope[j]).astype(BF16)
        own.p1[j] = pre1_grad
        own.grad_r[...] += nt(pre1_grad, own.t_all[j, 1])

    def backward_heads(j):
        own.grad_h[...] += nt(own.p1[j], own.t_all[j, 0])

    def pick_heads(r, table):
        heads = nn(table, hot_rows(head_ids[r : r + 1, :], ENT))
        own.pic_h[...] = nn(heads.T.astype(BF16), space_ref[:D, :]).astype(BF16)

    def pick_relations(r, table):
        relations = nn(table, hot_rows(rel_ids[r : r + 1, :], REL))
        own.pic_r[...] = nn(relations.T.astype(BF16), space_ref[:D, :]).astype(BF16)

    def rows_go(r, table):
        b = rounds[r]
        rows = nn(table, hot_rows(own.negs_in[r, r : r + 1, :], ENT)).T.astype(BF16)
        b.pick_neg[...] = nn(rows, widen()).astype(BF16)
        rows = nn(table, hot_rows(own.tails_in[r, r : r + 1, :], ENT)).T.astype(BF16)
        b.pick_tail[...] = nn(rows, widen()).astype(BF16)
        slot = b.negs.at[c, y_lo, z]
        return (
            [copies.start(b.pick_neg, slot, across[r](i)) for i in zs + [z]],
            copies.start(b.pick_tail, b.tails, partners[r]),
        )

    def negs_beside(r):
        half = rounds[r].negs.at[c, y_lo]
        return copies.start(half, half, beside)

    def negs_to_mate(r):
        half = rounds[r].negs.at[c]
        return copies.start(half, half, mate)

    loop(0, 4, build)
    all_here()
    asked = [
        (
            copies.start(tail_ids, own.tails_in.at[r], partners[r]),
            copies.start(neg_ids, own.negs_in.at[r], partners[r]),
        )
        for r in range(2)
    ]
    ent_copy.wait()
    table = own.ent[...].astype(BF16)
    pick_heads(0, table)
    loop(4, 7, build)
    for pair in asked:
        wait_all(pair)
    along, tail_go = rows_go(0, table)
    loop(7, STEPS, build)
    rel_copy.wait()
    pick_relations(0, own.rel[...].astype(BF16))
    wait_all(w_copies)
    own.acc[...] = jnp.zeros_like(own.acc)
    triples(0, 6, forward)
    wait_all(along)
    near = negs_beside(0)
    triples(6, STEPS, forward)
    near.wait()
    near = negs_to_mate(0)
    near.wait()
    tail_go.wait()

    for r in range(2):
        b = rounds[r]
        more = r == 0
        if r == 1:
            own.acc[...] = jnp.zeros_like(own.acc)
            triples(0, STEPS, lambda j: forward(j, own.slope))
            near.wait()
            tail_go.wait()
        pre2 = own.acc[...] + fc_bias[...]
        sigma = jax.nn.sigmoid(pre2)
        query = nn((pre2 * sigma).astype(BF16), widen()).astype(BF16)
        tails = b.tails[...].astype(F32)
        wide = query.astype(F32)
        pos_grad = -jax.nn.sigmoid(-jnp.sum(wide * tails, axis=1, keepdims=True))
        negset = b.negs[...].reshape(1024, LANES)
        by_neg = (negative_weight * jax.nn.sigmoid(nt(negset, query))).astype(BF16)
        b.neg_part[...] = nn(by_neg, query).astype(BF16).reshape(2, 2, 8, NEG, LANES)
        b1_copy = copies.start(b.neg_part.at[1 - c], b.b1, mate)
        b.tail_grad[...] = (pos_grad * wide).T[:D]
        tail_copy = copies.start(b.tail_grad, b.tail_in, partners[r])
        by_row = (negative_weight * jax.nn.sigmoid(nt(query, negset))).astype(BF16)
        query_grad = (pos_grad * tails + nn(by_row, negset))[:, :D]
        own.pre2_grad[...] = (query_grad * (sigma * (1.0 + pre2 * (1.0 - sigma)))).astype(BF16)
        own.grad_h[...] = jnp.zeros_like(own.grad_h)
        own.grad_r[...] = jnp.zeros_like(own.grad_r)
        triples(0, 3, backward)
        b1_copy.wait()
        b.b2_send[...] = (b.neg_part[c, 1 - y_lo].astype(F32) + b.b1[1 - y_lo].astype(F32)).astype(BF16)
        b2_copy = copies.start(b.b2_send, b.b2_recv, beside)
        triples(3, STEPS, backward)
        relation_grad = spread_nt_right(own.grad_r[...], space_ref[...])
        rel_row = rel_ids[r : r + 1, :]
        half = REL_PAD // 2

        def part_of(core):
            where = lax.broadcasted_iota(jnp.int32, (half, TRI), 0) + core * half
            hot = jnp.where(where == rel_row, 1.0, 0.0).astype(BF16)
            return spread_dot(hot, relation_grad).reshape(4, 4, BLK, LANES)

        b.s0_send[...] = part_of(1 - c).astype(BF16)
        s0_copy = copies.start(b.s0_send, b.s0_recv, mate)
        own.own_part[...] = part_of(c)
        s0_copy.wait()
        joined = own.own_part[...] + b.s0_recv[...].astype(F32)
        own.own_part[...] = joined
        s1_copies = []
        for h in range(2):
            b.s1_send[h] = joined[..., h * 128 : h * 128 + 128].astype(BF16)
            s1_copies.append(
                [
                    copies.start(b.s1_send.at[h, i, k], b.s1_recv.at[h, d], me.at(x=i, y=k))
                    for d, (i, k) in enumerate(plane)
                ]
            )
        b2_copy.wait()
        b.b3_send[...] = (
            b.neg_part[c, y_lo].astype(F32) + b.b1[y_lo].astype(F32) + b.b2_recv[...].astype(F32)
        ).astype(BF16)
        b3_copies = [
            copies.start(b.b3_send.at[i], b.b3_recv.at[d], me.at(z=i)) for d, i in enumerate(zs)
        ]
        triples(0, STEPS, backward_heads)
        head_grad = spread_nt(space_ref[:D, :], own.grad_h[...])
        own.ent_grad[...] = spread_nt_right(head_grad, hot_rows(head_ids[r : r + 1, :], ENT))
        wait_all(b3_copies)
        share = b.b3_send[z].astype(F32)
        for d in range(7):
            share = share + b.b3_recv[d].astype(F32)
        b.b4_send[...] = share
        b4_copy = copies.start(b.b4_send, b.b4_recv, partners[r])
        z_copies = []
        for h in range(2):
            wait_all(s1_copies[h])
            mine = own.own_part[me.x, me.y][:, h * 128 : h * 128 + 128]
            for d in range(15):
                mine = mine + b.s1_recv[h, d].astype(F32)
            b.z_buf[h, z] = mine.astype(BF16)
            slot = b.z_buf.at[h, z]
            z_copies.append([copies.start(slot, slot, me.at(z=i)) for i in zs])
        tail_copy.wait()
        own.ent_grad[...] += spread_nt_right(b.tail_in[...], hot_rows(own.tails_in[r, r : r + 1, :], ENT))
        b4_copy.wait()
        gradient = own.ent_grad[...] + spread_nt_right(
            b.b4_recv[...].T[:D], hot_rows(own.negs_in[r, r : r + 1, :], ENT)
        )
        new_rows, new_state = step_of(own.ent[...], (ent_state_in if more else ent_state)[...], gradient)
        own.ent[...] = new_rows
        ent_state[...] = new_state
        if not more:
            ent_copy = pltpu.make_async_copy(own.ent, ent_out, w_sem.at[STEPS])
            ent_copy.start()
        if more:
            table = own.ent[...].astype(BF16)
            along, tail_go = rows_go(1, table)
        s4_copies = []
        for h in range(2):
            wait_all(z_copies[h])
            total = b.z_buf[h, 0].astype(F32)
            for i in range(1, 8):
                total = total + b.z_buf[h, i].astype(F32)
            b.g_buf[h, c, me.x, me.y] = total.astype(BF16)
            slot = b.g_buf.at[h, c, me.x, me.y]
            s4_copies.append([copies.start(slot, slot, me.at(x=i, y=k)) for i, k in plane])
        if more:
            pick_heads(1, table)
            triples(0, STEPS, forward_heads)
            wait_all(along)
            near = negs_beside(1)
        s6_copies = []
        for h in range(2):
            wait_all(s4_copies[h])
            slot = b.g_buf.at[h, c]
            s6_copies.append(copies.start(slot, slot, mate))
        if more:
            near.wait()
            near = negs_to_mate(1)
        wait_all(s6_copies)
        wide = widen()
        gradient = (
            nt(wide[:, :128], b.g_buf[0].reshape(REL_PAD, 128)) + nt(wide[:, 128:], b.g_buf[1].reshape(REL_PAD, 128))
        )[:, :REL]
        old_state = (rel_state_in if more else rel_state)[...].reshape(1, REL)
        new_rows, new_state = step_of(own.rel[...], old_state, gradient)
        if more:
            own.rel[...] = new_rows
        else:
            rel[...] = new_rows
            ent_copy.wait()
        rel_state[...] = new_state.reshape(REL)
        if more:
            pick_relations(1, new_rows.astype(BF16))


def shards(
    entity_rows, entity_state, relation_rows, relation_state,
    conv_weight, conv_bias, fc_weight, fc_bias,
    head_ids, rel_ids, tail_ids, neg_ids,
):
    vmem = pl.BlockSpec(memory_space=pltpu.VMEM)
    operands = [
        head_ids, rel_ids, tail_ids, neg_ids,
        entity_rows.T, entity_state.reshape(1, ENT), relation_rows.T, relation_state,
        jnp.transpose(conv_weight, (1, 2, 0)), conv_bias.reshape(1, FILTERS),
        fc_weight.T, fc_bias.reshape(1, D), features(), spacing(),
    ]
    specs = [vmem] * len(operands)
    far = pl.BlockSpec(memory_space=pltpu.HBM)
    specs[4] = specs[6] = specs[10] = far
    ent, ent_state, rel, rel_state = pl.pallas_call(
        window_kernel,
        out_shape=(
            jax.ShapeDtypeStruct((D, ENT), F32),
            jax.ShapeDtypeStruct((1, ENT), F32),
            jax.ShapeDtypeStruct((D, REL), F32),
            jax.ShapeDtypeStruct((REL,), F32),
        ),
        in_specs=specs,
        out_specs=(far, vmem, vmem, vmem),
        scratch_shapes=[
            *SHARED_SCRATCH.values(),
            *ROUND_SCRATCH.values(),
            *ROUND_SCRATCH.values(),
            pltpu.SemaphoreType.DMA((STEPS + 2,)),
            pltpu.SemaphoreType.DMA((COPIES,)),
            pltpu.SemaphoreType.DMA((COPIES,)),
        ],
        compiler_params=pltpu.CompilerParams(
            collective_id=0, has_side_effects=True, vmem_limit_bytes=60 << 20
        ),
        name="window",
    )(*operands)
    return ent.T, ent_state.reshape(ENT), rel.T, rel_state


def solution(mesh):
    both = ("group", "shard")
    in_specs = (
        P(both, None), P(both), P(), P(), P(), P(), P(), P(),
        P(None, both), P(None, both), P(None, both), P(None, both),
    )
    out_specs = (P(both, None), P(both), P(), P())
    return jax.shard_map(shards, mesh=mesh, in_specs=in_specs, out_specs=out_specs, check_vma=False)
```
